256 devices in a mesh: clip: 16 (over z_hi, x), frame: 16 (over y, z_lo, core).
Axes of the slice: x: 4, y: 4, z: 8 (z_hi: 4, z_lo: 2; z = z_hi * 2 + z_lo), core: 2. Of those that a mesh axis runs over, the one named last changes fastest.
Arguments:
- frames_in: bfloat16 [16, 32, 96, 1280], P('clip', 'frame'), may hold values from -6 to 6
- ref_feats: bfloat16 [16, 96, 1280], P('clip', 'frame'), may hold values from -6 to 6
- out_grad: bfloat16 [16, 32, 96, 1280], P('clip', 'frame'), may hold values from -6 to 6
- space_query: bfloat16 [1280, 640], P('frame'), may hold values from -0.15625 to 0.15625
- space_key: bfloat16 [1280, 640], P('frame'), may hold values from -0.15625 to 0.15625
- space_value: bfloat16 [1280, 640], P('frame'), may hold values from -0.15625 to 0.15625
- space_output: bfloat16 [640, 1280], P('frame'), may hold values from -0.25 to 0.25
- time_query: bfloat16 [1280, 640], P('frame'), may hold values from -0.15625 to 0.15625
- time_key: bfloat16 [1280, 640], P('frame'), may hold values from -0.15625 to 0.15625
- time_value: bfloat16 [1280, 640], P('frame'), may hold values from -0.15625 to 0.15625
- time_output: bfloat16 [640, 1280], P('frame'), may hold values from -0.25 to 0.25
Outputs:
- out: bfloat16 [16, 32, 96, 1280], P('clip', 'frame')
- frames_grad: bfloat16 [16, 32, 96, 1280], P('clip', 'frame')
- ref_grad: bfloat16 [16, 96, 1280], P('clip', 'frame')
- space_query_grad: float32 [1280, 640], P('frame')
- space_key_grad: float32 [1280, 640], P('frame')
- space_value_grad: float32 [1280, 640], P('frame')
- space_output_grad: float32 [640, 1280], P('frame')
- time_query_grad: float32 [1280, 640], P('frame')
- time_key_grad: float32 [1280, 640], P('frame')
- time_value_grad: float32 [1280, 640], P('frame')
- time_output_grad: float32 [640, 1280], P('frame')
The draws below stay inside these ranges and needn't reach their ends.
All inputs are finite; a program needn't handle non-finite values.
Results may differ from the reference program's by a relative error of at most 0.035.
Values may be sent and summed in bfloat16 or wider, within the bound.
A program may use at most 128 MiB of HBM per device.

```python
import math
import jax
import jax.numpy as jnp
from jax import lax

D = 1280
HEADS = 4
S = 96
FR_DEV = 2
INNER = 640
FRAMES = 32
CLIPS = 16
BLOCKS = 16
REF_DEV = 6


def level_of(rng, dims, shards, least, largest):
    level = 1.0
    for position, blocks in shards:
        steps = jax.random.uniform(jax.random.fold_in(jax.random.fold_in(rng, 6), position), (blocks,), jnp.float32, least / len(shards), largest / len(shards))
        level = level * jnp.repeat(jnp.exp(steps), dims[position] // blocks).reshape((-1,) + (1,) * (len(dims) - 1 - position))
    return level


def normal_values(key, shape, deviation, reach, shards=(), held_as=jnp.bfloat16):
    loudness = level_of(key, shape, shards, -0.22, 0.18) if shards else 1.0
    values = jax.random.normal(key, shape, jnp.float32) * deviation * loudness
    return jnp.minimum(jnp.maximum(values, -reach), reach).astype(held_as)


def setup_inputs(seed: int = 0) -> dict:
    arg_keys = jax.random.split(jax.random.key(seed), 12)
    return {
        "frames_in": normal_values(arg_keys[0], (CLIPS, FRAMES, S, D), 1.0, 6.0, ((0, 16), (1, 16))),
        "ref_feats": normal_values(arg_keys[1], (CLIPS, S, D), 1.0, 6.0, ((0, 16), (1, 16))),
        "out_grad": normal_values(arg_keys[2], (CLIPS, FRAMES, S, D), 1.0, 6.0, ((0, 16), (1, 16))),
        "space_query": normal_values(arg_keys[3], (D, INNER), D ** -0.5, 0.15625, ((0, 16),)),
        "space_key": normal_values(arg_keys[4], (D, INNER), D ** -0.5, 0.15625, ((0, 16),)),
        "space_value": normal_values(arg_keys[5], (D, INNER), D ** -0.5, 0.15625, ((0, 16),)),
        "space_output": normal_values(arg_keys[6], (INNER, D), INNER ** -0.5, 0.25, ((0, 16),)),
        "time_query": normal_values(arg_keys[7], (D, INNER), D ** -0.5, 0.15625, ((0, 16),)),
        "time_key": normal_values(arg_keys[8], (D, INNER), D ** -0.5, 0.15625, ((0, 16),)),
        "time_value": normal_values(arg_keys[9], (D, INNER), D ** -0.5, 0.15625, ((0, 16),)),
        "time_output": normal_values(arg_keys[10], (INNER, D), INNER ** -0.5, 0.25, ((0, 16),)),
    }


EPSILON = 1e-05

def layer_stats(rows):
    wide = rows.astype(jnp.float32)
    centre = lax.optimization_barrier(jnp.mean(wide, -1, keepdims=True))
    offset = wide - centre
    inverse = lax.rsqrt(lax.optimization_barrier(jnp.mean(offset * offset, -1, keepdims=True)) + EPSILON)
    return (offset * inverse, inverse)

def layer_back(centred, inverse, cotangent):
    first = lax.optimization_barrier(jnp.mean(cotangent, -1, keepdims=True))
    second = lax.optimization_barrier(jnp.mean(cotangent * centred, -1, keepdims=True))
    return inverse * (cotangent - first - centred * second)

def position_table(first, count, width):
    frame_ids = (first + jnp.arange(count, dtype=jnp.int32)).astype(jnp.float32)
    halves = jnp.arange(width // 2, dtype=jnp.int32).astype(jnp.float32)
    rates = jnp.exp(halves * (-2.0 * math.log(10000.0) / width))
    angles = frame_ids[:, None] * rates[None, :]
    return jnp.stack([jnp.sin(angles), jnp.cos(angles)], -1).reshape(count, width)

def einsum_forms(temporal):
    if temporal:
        return ('qbhe,kbhe->bhqk', 'bhqk,kbhe->qbhe', 'bhqk,qbhe->kbhe')
    return ('bqhe,bkhe->bhqk', 'bhqk,bkhe->bqhe', 'bhqk,bqhe->bkhe')

def product(form, left, right):
    return jnp.einsum(form, left.astype(jnp.float32), right.astype(jnp.float32))

def attention(query, keys, values, temporal):
    score_form, mix_form, back_form = einsum_forms(temporal)
    scores = product(score_form, query, keys) * query.shape[-1] ** (-0.5)
    powers = jnp.exp(scores)
    probs = powers / lax.optimization_barrier(jnp.sum(powers, -1, keepdims=True))
    rounded = probs.astype(jnp.bfloat16)
    mixed = product(mix_form, rounded, values).astype(jnp.bfloat16)
    return (mixed, probs, rounded)

def attention_back(query, keys, values, probs, rounded, cotangent, temporal):
    score_form, mix_form, back_form = einsum_forms(temporal)
    prob_grad = product(score_form, cotangent, values)
    score_grad = probs * (prob_grad - lax.optimization_barrier(jnp.sum(probs * prob_grad, -1, keepdims=True)))
    score_rounded = (score_grad * query.shape[-1] ** (-0.5)).astype(jnp.bfloat16)
    query_grad = product(mix_form, score_rounded, keys).astype(jnp.bfloat16)
    key_grad = product(back_form, score_rounded, query)
    value_grad = product(back_form, rounded, cotangent)
    return (query_grad, key_grad, value_grad)

def split_heads(rows):
    return rows.reshape(rows.shape[:-1] + (HEADS, rows.shape[-1] // HEADS))

def merge_heads(rows):
    return rows.reshape(rows.shape[:-2] + (rows.shape[-2] * rows.shape[-1],))

def project(rows, weight):
    flat_rows = rows.reshape(-1, rows.shape[-1])
    result = jnp.dot(flat_rows, weight, preferred_element_type=jnp.float32)
    return result.reshape(rows.shape[:-1] + (weight.shape[1],))

def project_back(rows, weight):
    flat_rows = rows.reshape(-1, rows.shape[-1])
    result = lax.dot_general(flat_rows, weight, (((1,), (1,)), ((), ())), preferred_element_type=jnp.float32)
    return result.reshape(rows.shape[:-1] + (weight.shape[0],))

def outer_sum(left, right):
    left_rows = left.reshape(-1, left.shape[-1])
    right_rows = right.reshape(-1, right.shape[-1])
    return lax.dot_general(left_rows, right_rows, (((0,), (0,)), ((), ())), preferred_element_type=jnp.float32)

def reference(frames_in, ref_feats, out_grad, space_query, space_key, space_value, space_output, time_query, time_key, time_value, time_output):
    table = position_table(0, FRAMES, D)

    def one_clip(carry, data):
        frames, refer, cotangent = data
        centred_one, inverse_one = layer_stats(frames)
        normed_one = centred_one.astype(jnp.bfloat16)
        spatial_query = project(normed_one, space_query).astype(jnp.bfloat16)
        spatial_key = project(normed_one, space_key).astype(jnp.bfloat16)
        spatial_value = project(normed_one, space_value).astype(jnp.bfloat16)
        refer_key = project(refer, space_key).astype(jnp.bfloat16)
        refer_value = project(refer, space_value).astype(jnp.bfloat16)
        keys_joined = jnp.concatenate([spatial_key, jnp.broadcast_to(refer_key[None], spatial_key.shape)], 1)
        values_joined = jnp.concatenate([spatial_value, jnp.broadcast_to(refer_value[None], spatial_value.shape)], 1)
        spatial_mixed, spatial_probs, spatial_rounded = attention(split_heads(spatial_query), split_heads(keys_joined), split_heads(values_joined), False)
        spatial_mixed = merge_heads(spatial_mixed)
        hidden_one = (frames.astype(jnp.float32) + project(spatial_mixed, space_output)).astype(jnp.bfloat16)
        centred_two, inverse_two = layer_stats(hidden_one)
        normed_two = (centred_two + table[:, None, :]).astype(jnp.bfloat16)
        temporal_query = project(normed_two, time_query).astype(jnp.bfloat16)
        temporal_key = project(normed_two, time_key).astype(jnp.bfloat16)
        temporal_value = project(normed_two, time_value).astype(jnp.bfloat16)
        temporal_mixed, temporal_probs, temporal_rounded = attention(split_heads(temporal_query), split_heads(temporal_key), split_heads(temporal_value), True)
        temporal_mixed = merge_heads(temporal_mixed)
        output = (hidden_one.astype(jnp.float32) + project(temporal_mixed, time_output)).astype(jnp.bfloat16)
        mixed_grad_two = project_back(cotangent, time_output).astype(jnp.bfloat16)
        query_grad_two, key_grad_two, value_grad_two = attention_back(split_heads(temporal_query), split_heads(temporal_key), split_heads(temporal_value), temporal_probs, temporal_rounded, split_heads(mixed_grad_two), True)
        query_grad_two = merge_heads(query_grad_two)
        key_grad_two = merge_heads(key_grad_two).astype(jnp.bfloat16)
        value_grad_two = merge_heads(value_grad_two).astype(jnp.bfloat16)
        normed_grad_two = project_back(query_grad_two, time_query) + project_back(key_grad_two, time_key) + project_back(value_grad_two, time_value)
        hidden_grad = (cotangent.astype(jnp.float32) + layer_back(centred_two, inverse_two, normed_grad_two)).astype(jnp.bfloat16)
        mixed_grad_one = project_back(hidden_grad, space_output).astype(jnp.bfloat16)
        query_grad_one, key_joined_grad, value_joined_grad = attention_back(split_heads(spatial_query), split_heads(keys_joined), split_heads(values_joined), spatial_probs, spatial_rounded, split_heads(mixed_grad_one), False)
        query_grad_one = merge_heads(query_grad_one)
        key_grad_one = merge_heads(key_joined_grad[:, :S]).astype(jnp.bfloat16)
        value_grad_one = merge_heads(value_joined_grad[:, :S]).astype(jnp.bfloat16)
        refer_key_grad = merge_heads(lax.optimization_barrier(jnp.sum(key_joined_grad[:, S:], 0))).astype(jnp.bfloat16)
        refer_value_grad = merge_heads(lax.optimization_barrier(jnp.sum(value_joined_grad[:, S:], 0))).astype(jnp.bfloat16)
        normed_grad_one = project_back(query_grad_one, space_query) + project_back(key_grad_one, space_key) + project_back(value_grad_one, space_value)
        frames_grad = (hidden_grad.astype(jnp.float32) + layer_back(centred_one, inverse_one, normed_grad_one)).astype(jnp.bfloat16)
        refer_grad = (project_back(refer_key_grad, space_key) + project_back(refer_value_grad, space_value)).astype(jnp.bfloat16)

        def add_block(block, sums):
            start = (block * FR_DEV).astype(jnp.int32)
            ref_start = (block * REF_DEV).astype(jnp.int32)

            def rows(array):
                return lax.dynamic_slice_in_dim(array, start, FR_DEV, 0)

            def ref_rows(array):
                return lax.dynamic_slice_in_dim(array, ref_start, REF_DEV, 0)
            normed_block = rows(normed_one)
            second_block = rows(normed_two)
            terms = (outer_sum(normed_block, rows(query_grad_one)), outer_sum(normed_block, rows(key_grad_one)) + outer_sum(ref_rows(refer), ref_rows(refer_key_grad)), outer_sum(normed_block, rows(value_grad_one)) + outer_sum(ref_rows(refer), ref_rows(refer_value_grad)), outer_sum(rows(spatial_mixed), rows(hidden_grad)), outer_sum(second_block, rows(query_grad_two)), outer_sum(second_block, rows(key_grad_two)), outer_sum(second_block, rows(value_grad_two)), outer_sum(rows(temporal_mixed), rows(cotangent)))
            return tuple((total + lax.optimization_barrier(term.astype(jnp.bfloat16)).astype(jnp.float32) for total, term in zip(sums, terms)))
        carry = lax.fori_loop(0, BLOCKS, add_block, carry)
        return (carry, (output, frames_grad, refer_grad))
    wide = jnp.zeros((D, INNER), jnp.float32)
    tall = jnp.zeros((INNER, D), jnp.float32)
    start_sums = (wide, wide, wide, tall, wide, wide, wide, tall)
    grads, (output, frames_grad, refer_grad) = lax.scan(one_clip, start_sums, (frames_in, ref_feats, out_grad))
    return (output, frames_grad, refer_grad, grads[0], grads[1], grads[2], grads[3], grads[4], grads[5], grads[6], grads[7])
```

```python
import math

import jax
import jax.numpy as jnp
from jax import lax
from jax.experimental import pallas as pl
from jax.experimental.pallas import tpu as pltpu
from jax.sharding import PartitionSpec as P


MESH = pl.DeviceIdType.MESH
ANY = pl.BlockSpec(memory_space=pl.ANY)
VM = pl.BlockSpec(memory_space=pltpu.VMEM)


class Place:
    def __init__(self):
        clip, frame = lax.axis_index("clip"), lax.axis_index("frame")
        self.clip, self.frame = clip, frame
        self.x, self.zh = lax.rem(clip, 4), lax.div(clip, 4)
        self.y, self.zl, self.core = lax.div(frame, 4), lax.rem(lax.div(frame, 2), 2), lax.rem(frame, 2)
        self.parity = lax.rem(self.x, 2)
        self.sibling = (clip, frame + 1 - 2 * self.core)

    def along_y(self, step):
        return (self.clip, lax.rem(self.y + 4 + step, 4) * 4 + self.zl * 2 + self.core)

    def along_x(self, step):
        return (self.zh * 4 + lax.rem(self.x + 4 + step, 4), self.frame)

    def along_z(self, step):
        far = lax.rem(self.zh * 2 + self.zl + 8 + step, 8)
        return (lax.div(far, 2) * 4 + self.x, self.y * 4 + lax.rem(far, 2) * 2 + self.core)

    def along_zh(self, step):
        return (lax.rem(self.zh + 4 + step, 4) * 4 + self.x, self.frame)

    def peer(self, step):
        return (self.clip, lax.rem(self.frame + step, 16))


def greet(devices):
    barrier = pltpu.get_barrier_semaphore()
    for device in devices:
        pl.semaphore_signal(barrier, inc=1, device_id=device, device_id_type=MESH)
    pl.semaphore_wait(barrier, len(devices))


def remote(src, dst, send, recv, device):
    return pltpu.make_async_remote_copy(
        src_ref=src, dst_ref=dst, send_sem=send, recv_sem=recv, device_id=device, device_id_type=MESH)


def shard_of(y, zl, core):
    return lax.rem(y + 8, 4) * 4 + zl * 2 + core


def gather_kernel(pack, ref8, full, refs, sib_s, sib_r, y_s, y_r, rel_s, rel_r, z_s, z_r, x_s, x_r, ref_s, ref_r, loc):
    at = Place()
    y, zl, core, p, me = at.y, at.zl, at.core, at.parity, at.frame
    greet([at.along_x(1), at.along_x(-1), at.along_z(1), at.along_z(-1)] + [at.peer(i) for i in range(1, 16)])
    sends = []

    def go(copy):
        copy.start()
        sends.append(copy)

    def pair(j):
        return pl.ds(2 * j, 2)

    steps = (1, -1)
    own = [[None] * 4 for _ in steps]
    for j in range(4):
        for s, step in enumerate(steps):
            own[s][j] = remote(pack.at[pair(j)], full.at[me, pair(j)], y_s.at[s, j], y_r.at[s, j], at.along_y(step))

    def z_copy(k, h, d, src):
        w = 4 * h + 2 * p + d
        return remote(src, full.at[shard_of(y + k, zl, core), w], z_s.at[k, h, d], z_r.at[k, h, d],
                      at.along_z(1 - 2 * d))

    sib_count = [0]

    def to_sibling(index, src, dst):
        go(remote(src, dst, sib_s.at[index], sib_r.at[index], at.sibling))

    for j in range(2):
        for s in range(2):
            go(own[s][j])
    for d in range(2):
        go(z_copy(0, 0, d, pack.at[2 * p + d]))
    for j in range(2, 4):
        for s in range(2):
            go(own[s][j])
    for d in range(2):
        go(z_copy(0, 1, d, pack.at[4 + 2 * p + d]))
    to_sibling(0, pack, full.at[me])
    keep = pltpu.make_async_copy(pack, full.at[me], loc.at[0])
    keep.start()
    keep_ref = pltpu.make_async_copy(ref8, refs.at[me], loc.at[1])
    keep_ref.start()
    for i in range(1, 16):
        go(remote(ref8, refs.at[me], ref_s.at[i], ref_r.at[i], at.peer(i)))

    def y_wait(s, j):
        src = shard_of(y - steps[s], zl, core)
        ref = full.at[src, pair(j)]
        remote(ref, ref, y_s.at[s, j], y_r.at[s, j], at.along_y(steps[s])).wait_recv()
        to_sibling(1 + s * 4 + j, ref, ref)
        if j % 2 == s:
            go(remote(ref, ref, rel_s.at[j], rel_r.at[j], at.along_y(steps[s])))

    def rel_wait(j):
        ref = full.at[shard_of(y + 2, zl, core), pair(j)]
        remote(ref, ref, rel_s.at[j], rel_r.at[j], at.along_y(1)).wait_recv()
        to_sibling(9 + j, ref, ref)

    def z_send(k, h):
        for d in range(2):
            go(z_copy(k, h, d, full.at[shard_of(y + k, zl, core), 4 * h + 2 * p + d]))

    def z_wait(k, h):
        for d in range(2):
            ref = full.at[shard_of(y + k, 1 - zl, core), 4 * h + 2 * p + d]
            remote(ref, ref, z_s.at[k, h, d], z_r.at[k, h, d], at.along_z(1)).wait_recv()
            go(remote(ref, ref, x_s.at[k, h, d], x_r.at[k, h, d], at.along_x(1 - 2 * d)))
            to_sibling(13 + (k * 2 + h) * 2 + d, ref, ref)

    def x_wait(k, h):
        for d in range(2):
            ref = full.at[shard_of(y + k, 1 - zl, core), 4 * h + 2 * (1 - p) + d]
            remote(ref, ref, x_s.at[k, h, d], x_r.at[k, h, d], at.along_x(1)).wait_recv()
            to_sibling(29 + (k * 2 + h) * 2 + d, ref, ref)

    for h in range(2):
        for j in (2 * h, 2 * h + 1):
            for s in range(2):
                y_wait(s, j)
        z_send(1, h)
        z_send(3, h)
        z_wait(0, h)
        for j in (2 * h, 2 * h + 1):
            rel_wait(j)
        z_send(2, h)
        z_wait(1, h)
        z_wait(3, h)
        x_wait(0, h)
        z_wait(2, h)
        x_wait(1, h)
        x_wait(3, h)
        x_wait(2, h)

    other = 1 - core

    def sib_wait(index, ref):
        remote(ref, ref, sib_s.at[index], sib_r.at[index], at.sibling).wait_recv()

    sib_wait(0, full.at[shard_of(y, zl, other)])
    for s in range(2):
        for j in range(4):
            sib_wait(1 + s * 4 + j, full.at[shard_of(y - steps[s], zl, other), pair(j)])
    for j in range(4):
        sib_wait(9 + j, full.at[shard_of(y + 2, zl, other), pair(j)])
    for k in range(4):
        for h in range(2):
            for d in range(2):
                i = (k * 2 + h) * 2 + d
                dst = shard_of(y + k, 1 - zl, other)
                sib_wait(13 + i, full.at[dst, 4 * h + 2 * p + d])
                sib_wait(29 + i, full.at[dst, 4 * h + 2 * (1 - p) + d])
    for i in range(1, 16):
        ref = refs.at[lax.rem(me + 16 - i, 16)]
        remote(ref, ref, ref_s.at[i], ref_r.at[i], at.peer(i)).wait_recv()
    for copy in sends:
        copy.wait_send()
    keep.wait()
    keep_ref.wait()


def gather(pack, ref8):
    dma = pltpu.SemaphoreType.DMA
    return pl.pallas_call(
        gather_kernel,
        out_shape=(jax.ShapeDtypeStruct((16, 8, 80, 640), jnp.bfloat16),
                   jax.ShapeDtypeStruct((16, 8, 1280), jnp.bfloat16)),
        in_specs=[VM, VM],
        out_specs=(ANY, ANY),
        scratch_shapes=[dma((45,)), dma((45,)), dma((2, 4)), dma((2, 4)), dma((4,)), dma((4,)),
                        dma((4, 2, 2)), dma((4, 2, 2)), dma((4, 2, 2)), dma((4, 2, 2)), dma((16,)), dma((16,)),
                        dma((2,))],
        compiler_params=pltpu.CompilerParams(collective_id=0, has_side_effects=True),
        name="gather_weights",
    )(pack, ref8)

BF, F32 = jnp.bfloat16, jnp.float32
EPSILON = 1e-05
SCALE = 160 ** -0.5


def dot(a, b, ca=1, cb=0):
    return lax.dot_general(a, b, (((ca,), (cb,)), ((), ())), preferred_element_type=F32)


def stats(wide):
    offset = wide - jnp.mean(wide, -1, keepdims=True)
    inverse = lax.rsqrt(jnp.mean(offset * offset, -1, keepdims=True) + EPSILON)
    return offset * inverse, inverse


def stats_back(centred, inverse, g):
    first = jnp.mean(g, -1, keepdims=True)
    second = jnp.mean(g * centred, -1, keepdims=True)
    return inverse * (g - first - centred * second)


def iota(shape, dim):
    return lax.broadcasted_iota(jnp.int32, shape, dim)


def one_hot(hit):
    return jnp.where(hit, 1.0, 0.0).astype(BF)


def frame_pack():
    r, c = iota((256, 192), 0), iota((256, 192), 1)
    d, j = lax.shift_right_logical(r, 4), lax.bitwise_and(r, 15)
    a = jnp.where(j >= 6, 1, 0)
    return one_hot((j < 12) & (c == 90 * a + 6 * d + j))


def frame_unpack():
    c, r = iota((192, 256), 0), iota((192, 256), 1)
    d, j = lax.shift_right_logical(r, 4), lax.bitwise_and(r, 15)
    a = jnp.where(j >= 6, 1, 0)
    return one_hot((j < 12) & (c == 90 * a + 6 * d + j))


def token_unpack():
    m, r = iota((192, 256), 0), iota((192, 256), 1)
    t, f, a = lax.shift_right_logical(m, 5), lax.bitwise_and(lax.shift_right_logical(m, 1), 15), lax.bitwise_and(m, 1)
    return one_hot(r == 16 * f + 6 * a + t)


def token_pack():
    m, r = iota((256, 192), 1), iota((256, 192), 0)
    t, f, a = lax.shift_right_logical(m, 5), lax.bitwise_and(lax.shift_right_logical(m, 1), 15), lax.bitwise_and(m, 1)
    return one_hot(r == 16 * f + 6 * a + t)


def ref_unpack(rows, cols, swap=False):
    m, r = (iota((rows, cols), 0), iota((rows, cols), 1)) if not swap else (iota((rows, cols), 1), iota((rows, cols), 0))
    d, j = lax.shift_right_logical(r, 3), lax.bitwise_and(r, 7)
    return one_hot((j < 6) & (m == 6 * d + j))


def head_masks():
    lane = iota((1, 640), 1)
    return [(lane >= 160 * h) & (lane < 160 * (h + 1)) for h in range(4)]


def stack_heads(rows, masks):
    return jnp.concatenate([rows * one_hot(m) for m in masks], 0)


def merge_heads(stacked, masks):
    n = stacked.shape[0] // 4
    total = jnp.where(masks[0], stacked[:n], 0.0)
    for h in range(1, 4):
        total = jnp.where(masks[h], stacked[h * n:(h + 1) * n], total)
    return total


def softmax(stacked, keys, same=None):
    powers = jnp.exp(dot(stacked, keys, 1, 1) * SCALE)
    if same is not None:
        powers = jnp.where(same, powers, 0.0)
    return powers / jnp.sum(powers, -1, keepdims=True)


def score_back(probs, grads, values):
    dp = dot(grads, values, 1, 1)
    return (probs * (dp - jnp.sum(probs * dp, -1, keepdims=True)) * SCALE).astype(BF)


def wide_output(slot):
    wide = slot.astype(F32)
    left = wide[:, :40].reshape(640, 640).astype(BF)
    right = wide[:, 40:].reshape(640, 640).astype(BF)
    return left, right


def pack_output(left, right):
    return jnp.concatenate([left.reshape(16, 40, 640), right.reshape(16, 40, 640)], 1)


def store_term(dw, w, term):
    parts = term.reshape(4, 2, 2, 80, 640).astype(BF)
    for core in range(2):
        for zl in range(2):
            dw[core, zl, w] = parts[:, zl, core]


def exchange_start(at, src, dst, send, recv):
    copies = []
    for i in range(1, 16):
        to = lax.rem(at.frame + i, 16)
        copy = remote(src.at[pl.ds(pl.multiple_of(16 * to, 16), 16)],
                      dst.at[pl.ds(pl.multiple_of(16 * at.frame, 16), 16)], send.at[i], recv.at[i], at.peer(i))
        copy.start()
        copies.append(copy)
    own = pl.ds(pl.multiple_of(16 * at.frame, 16), 16)
    dst[own, :] = src[own, :]
    return copies


def load(src, dst, sem):
    copy = pltpu.make_async_copy(src, dst, sem)
    copy.start()
    return copy


def space_kernel(frames, refs, og, full, h1_o, qkv_o, rkv_o, o_o, h1r, ogr, wts, buf_a, buf_b, wsem, s_s, r_s):
    at = Place()
    loads = [load(full.at[:, i], wts.at[i], wsem.at[i]) for i in range(4)]
    greet([at.peer(i) for i in range(1, 16)])
    pack = frame_pack()
    buf_a[...] = dot(pack, og[...]).astype(BF)
    copies = exchange_start(at, buf_a, ogr, s_s.at[0], r_s.at[0])
    masks = head_masks()
    wide = frames[...].astype(F32)
    n1 = stats(wide)[0].astype(BF)
    ref = dot(ref_unpack(96, 128), refs[...]).astype(BF)
    loads[0].wait()
    q = dot(n1, wts[0].reshape(1280, 640)).astype(BF)
    loads[1].wait()
    w = wts[1].reshape(1280, 640)
    k, rk = dot(n1, w).astype(BF), dot(ref, w).astype(BF)
    loads[2].wait()
    w = wts[2].reshape(1280, 640)
    v, rv = dot(n1, w).astype(BF), dot(ref, w).astype(BF)
    for i, part in enumerate((q, k, v)):
        qkv_o[i] = part
    rkv_o[0] = rk
    rkv_o[1] = rv
    outs = []
    for a in range(2):
        rows = slice(96 * a, 96 * a + 96)
        keys = jnp.concatenate([k[rows], rk], 0)
        values = jnp.concatenate([v[rows], rv], 0)
        probs = softmax(stack_heads(q[rows], masks), keys).astype(BF)
        outs.append(merge_heads(dot(probs, values), masks))
    o = jnp.concatenate(outs, 0).astype(BF)
    o_o[...] = o
    loads[3].wait()
    left, right = wide_output(wts[3])
    h1 = (wide + jnp.concatenate([dot(o, left), dot(o, right)], 1)).astype(BF)
    h1_o[...] = h1
    buf_b[...] = dot(pack, h1).astype(BF)
    copies += exchange_start(at, buf_b, h1r, s_s.at[1], r_s.at[1])
    for copy in copies:
        copy.wait()


def space(frames, refs, og, full):
    dma = pltpu.SemaphoreType.DMA
    s = jax.ShapeDtypeStruct
    return pl.pallas_call(
        space_kernel,
        out_shape=(s((192, 1280), BF), s((3, 192, 640), BF), s((2, 96, 640), BF), s((192, 640), BF),
                   s((256, 1280), BF), s((256, 1280), BF)),
        in_specs=[VM, VM, VM, ANY],
        out_specs=(VM,) * 6,
        scratch_shapes=[pltpu.VMEM((4, 16, 80, 640), BF), pltpu.VMEM((256, 1280), BF), pltpu.VMEM((256, 1280), BF),
                        dma((4,)), dma((2, 16)), dma((2, 16))],
        compiler_params=pltpu.CompilerParams(collective_id=1, has_side_effects=True, vmem_limit_bytes=60 << 20),
        name="space_forward",
    )(frames, refs, og, full)


def time_kernel(h1r, ogr, table, full, back, dw, wts, buf, wsem, s_s, r_s):
    at = Place()
    loads = [load(full.at[:, 4 + i], wts.at[i], wsem.at[i]) for i in range(4)]
    greet([at.peer(i) for i in range(1, 16)])
    masks = head_masks()
    unpack = token_unpack()
    h1 = dot(unpack, h1r[...])
    og = dot(unpack, ogr[...]).astype(BF)
    centred, inverse = stats(h1)
    n2 = (centred + jnp.concatenate([table[...]] * 6, 0)).astype(BF)
    parts = []
    for i in range(3):
        loads[i].wait()
        parts.append(dot(n2, wts[i].reshape(1280, 640)).astype(BF))
    q, k, v = parts
    r, c = iota((768, 192), 0), iota((768, 192), 1)
    r = jnp.where(r >= 384, r - 384, r)
    r = jnp.where(r >= 192, r - 192, r)
    same = lax.shift_right_logical(r, 5) == lax.shift_right_logical(c, 5)
    qs = stack_heads(q, masks)
    probs = softmax(qs, k, same)
    pb = probs.astype(BF)
    o2 = merge_heads(dot(pb, v), masks).astype(BF)
    loads[3].wait()
    left, right = wide_output(wts[3])
    go = (dot(og[:, :640], left, 1, 1) + dot(og[:, 640:], right, 1, 1)).astype(BF)
    gs = stack_heads(go, masks)
    eb = score_back(probs, gs, v)
    gq = merge_heads(dot(eb, k), masks).astype(BF)
    gk = dot(eb, qs, 0, 0).astype(BF)
    gv = dot(pb, gs, 0, 0).astype(BF)
    grads = (gq, gk, gv)
    gn = dot(gq, wts[0].reshape(1280, 640), 1, 1)
    for i in (1, 2):
        gn = gn + dot(grads[i], wts[i].reshape(1280, 640), 1, 1)
    gh = (og.astype(F32) + stats_back(centred, inverse, gn)).astype(BF)
    pack = token_pack()
    buf[:, :1280] = dot(pack, gh).astype(BF)
    buf[:, 1280:] = dot(pack, o2).astype(BF)
    copies = exchange_start(at, buf, back, s_s, r_s)
    for i in range(3):
        store_term(dw, i, dot(n2, grads[i], 0, 0))
    store_term(dw, 3, pack_output(dot(o2, og[:, :640], 0, 0), dot(o2, og[:, 640:], 0, 0)))
    for copy in copies:
        copy.wait()


def temporal(h1r, ogr, table, full):
    dma = pltpu.SemaphoreType.DMA
    s = jax.ShapeDtypeStruct
    return pl.pallas_call(
        time_kernel,
        out_shape=(s((256, 1920), BF), s((2, 2, 4, 4, 80, 640), BF)),
        in_specs=[VM, VM, VM, ANY],
        out_specs=(VM, VM),
        scratch_shapes=[pltpu.VMEM((4, 16, 80, 640), BF), pltpu.VMEM((256, 1920), BF),
                        dma((4,)), dma((16,)), dma((16,))],
        compiler_params=pltpu.CompilerParams(collective_id=2, has_side_effects=True, vmem_limit_bytes=60 << 20),
        name="time_both",
    )(h1r, ogr, table, full)


def back_kernel(backr, frames, refs, h1, qkv, rkv, o_in, full, out_o, fg_o, dw, gr_o, wts, wsem):
    order = (7, 3, 0, 1, 2)
    loads = {i: load(full.at[:, i], wts.at[n], wsem.at[n]) for n, i in enumerate(order)}
    masks = head_masks()
    unpack = frame_unpack()
    gh = dot(unpack, backr[:, :1280]).astype(BF)
    o2 = dot(unpack, backr[:, 1280:]).astype(BF)
    loads[7].wait()
    left, right = wide_output(wts[0])
    out_o[...] = (h1[...].astype(F32) + jnp.concatenate([dot(o2, left), dot(o2, right)], 1)).astype(BF)
    loads[3].wait()
    left, right = wide_output(wts[1])
    go = (dot(gh[:, :640], left, 1, 1) + dot(gh[:, 640:], right, 1, 1)).astype(BF)
    rk, rv = rkv[0], rkv[1]
    gq, gk, gv = [], [], []
    grk = grv = None
    for a in range(2):
        rows = slice(96 * a, 96 * a + 96)
        keys = jnp.concatenate([qkv[1, rows], rk], 0)
        values = jnp.concatenate([qkv[2, rows], rv], 0)
        qs = stack_heads(qkv[0, rows], masks)
        gs = stack_heads(go[rows], masks)
        probs = softmax(qs, keys)
        eb = score_back(probs, gs, values)
        gq.append(merge_heads(dot(eb, keys), masks))
        gkeys = dot(eb, qs, 0, 0)
        gvalues = dot(probs.astype(BF), gs, 0, 0)
        gk.append(gkeys[:96])
        gv.append(gvalues[:96])
        grk = gkeys[96:] if grk is None else grk + gkeys[96:]
        grv = gvalues[96:] if grv is None else grv + gvalues[96:]
    gq, gk, gv = (jnp.concatenate(g, 0).astype(BF) for g in (gq, gk, gv))
    grk, grv = grk.astype(BF), grv.astype(BF)
    spread = ref_unpack(128, 96, True)
    gr_o[:, :640] = dot(spread, grk).astype(BF)
    gr_o[:, 640:] = dot(spread, grv).astype(BF)
    ref = dot(ref_unpack(96, 128), refs[...]).astype(BF)
    centred, inverse = stats(frames[...].astype(F32))
    n1 = centred.astype(BF)
    gn = None
    for n, (i, g) in enumerate(((0, gq), (1, gk), (2, gv))):
        loads[i].wait()
        term = dot(g, wts[2 + n].reshape(1280, 640), 1, 1)
        gn = term if gn is None else gn + term
    fg_o[...] = (gh.astype(F32) + stats_back(centred, inverse, gn)).astype(BF)
    store_term(dw, 0, dot(n1, gq, 0, 0))
    store_term(dw, 1, dot(n1, gk, 0, 0) + dot(ref, grk, 0, 0))
    store_term(dw, 2, dot(n1, gv, 0, 0) + dot(ref, grv, 0, 0))
    o = o_in[...]
    store_term(dw, 3, pack_output(dot(o, gh[:, :640], 0, 0), dot(o, gh[:, 640:], 0, 0)))


def back(backr, frames, refs, h1, qkv, rkv, o, full):
    dma = pltpu.SemaphoreType.DMA
    s = jax.ShapeDtypeStruct
    return pl.pallas_call(
        back_kernel,
        out_shape=(s((192, 1280), BF), s((192, 1280), BF), s((2, 2, 4, 4, 80, 640), BF), s((128, 1280), BF)),
        in_specs=[VM] * 7 + [ANY],
        out_specs=(VM,) * 4,
        scratch_shapes=[pltpu.VMEM((5, 16, 80, 640), BF), dma((5,))],
        compiler_params=pltpu.CompilerParams(vmem_limit_bytes=60 << 20),
        name="space_backward",
    )(backr, frames, refs, h1, qkv, rkv, o, full)


def add(*parts):
    total = parts[0].astype(F32)
    for part in parts[1:]:
        total = total + part.astype(F32)
    return total


def reduce_kernel(dws, dwt, gr, full, tot_sq, tot_sk, tot_sv, tot_so, tot_tq, tot_tk, tot_tv, tot_to, rg,
                  g, r0, rx, rz, ry1, ry2, pm, rax1, rax2, rq, fin, rgr, wts,
                  l_m, c_s, c_r, x_s, x_r, z_s, z_r, y1_s, y1_r, y2_s, y2_r,
                  a1_s, a1_r, a2_s, a2_r, q_s, q_r, g_s, g_r, gg_s, gg_r, e_s, e_r, w_m):
    at = Place()
    y, zl, p, x, zh, me = at.y, at.zl, at.parity, at.x, at.zh, at.frame
    core, oz = at.core, 1 - at.zl
    wloads = [load(full.at[:, 1 + i], wts.at[i], w_m.at[i]) for i in range(2)]
    halves = (dws, dwt)
    locals_ = {}
    for h in (1, 0):
        for a, zz in enumerate((oz, zl)):
            for w in range(4):
                locals_[h, a, w] = load(halves[h].at[core, zz, w], g.at[h, a, w], l_m.at[h, a, w])
    greet([at.peer(i) for i in range(1, 16)] + [at.along_x(1), at.along_x(-1), at.along_z(1), at.along_z(-1),
                                                at.along_zh(1), at.along_zh(-1), at.along_zh(2)])
    sends = []

    def go(copy):
        copy.start()
        sends.append(copy)
        return copy

    cross = {}
    for h in (1, 0):
        for a, zz in enumerate((oz, zl)):
            for w in range(4):
                cross[h, a, w] = go(remote(halves[h].at[1 - core, zz, w], r0.at[h, a, w], c_s.at[h, a, w],
                                           c_r.at[h, a, w], at.sibling))
    refs = []
    for i in range(1, 16):
        to = lax.rem(me + i, 16)
        refs.append(go(remote(gr.at[to], rgr.at[me], e_s.at[i], e_r.at[i], at.peer(i))))
    rgr[me] = gr[me]

    def rem4(v):
        return lax.rem(v + 8, 4)

    def chain(h):
        for a in range(2):
            for w in range(4):
                locals_[h, a, w].wait()
                cross[h, a, w].wait_recv()
                g[h, a, w] = add(g[h, a, w], r0[h, a, w]).astype(BF)
            if a == 0:
                xs = [go(remote(g.at[h, 0, 2 * (1 - p) + d], rx.at[h, d], x_s.at[h, d], x_r.at[h, d],
                                at.along_x(2 * d - 1))) for d in range(2)]
        yield
        zs = []
        for d in range(2):
            xs[d].wait_recv()
            w = 2 * p + d
            g[h, 0, w] = add(g[h, 0, w], rx[h, d]).astype(BF)
            zs.append(go(remote(g.at[h, 0, w], rz.at[h, d], z_s.at[h, d], z_r.at[h, d], at.along_z(2 * d - 1))))
        yield
        for d in range(2):
            zs[d].wait_recv()
            w = 2 * p + d
            g[h, 1, w] = add(g[h, 1, w], rz[h, d]).astype(BF)
        y1 = [go(remote(g.at[h, 1, w, rem4(y + 2)], ry1.at[h, w], y1_s.at[h, w], y1_r.at[h, w],
                        at.along_y(-1 if w < 2 else 1))) for w in range(4)]
        yield
        y2 = {}
        for w in range(4):
            y1[w].wait_recv()
            on = rem4(y + (-1 if w < 2 else 1))
            g[h, 1, w, on] = add(g[h, 1, w, on], ry1[h, w]).astype(BF)
            for s, step in enumerate((1, -1)):
                y2[s, w] = go(remote(g.at[h, 1, w, rem4(y + step)], ry2.at[s, h, w], y2_s.at[s, h, w],
                                     y2_r.at[s, h, w], at.along_y(step)))
        yield
        for w in range(4):
            y2[0, w].wait_recv()
            y2[1, w].wait_recv()
            pm[h, w] = add(g[h, 1, w, y], ry2[0, h, w], ry2[1, h, w]).astype(BF)
        low, high = pl.ds(0, 48), pl.ds(48, 32)
        far = rem4(x + 2)
        a1 = [go(remote(pm.at[h, far, part], rax1.at[h, part], a1_s.at[h, s], a1_r.at[h, s], at.along_x(step)))
              for s, (step, part) in enumerate(((1, low), (-1, high)))]
        yield
        for s, (step, part) in enumerate(((1, low), (-1, high))):
            a1[s].wait_recv()
            on = rem4(x + step)
            pm[h, on, part] = add(pm[h, on, part], rax1[h, part]).astype(BF)
        a2 = [go(remote(pm.at[h, rem4(x + step)], rax2.at[s, h], a2_s.at[s, h], a2_r.at[s, h], at.along_x(step)))
              for s, step in enumerate((1, -1))]
        yield
        for copy in a2:
            copy.wait_recv()
        rq[h, zh] = add(pm[h, x], rax2[0, h], rax2[1, h]).astype(BF)
        qs = [go(remote(rq.at[h, zh], rq.at[h, zh], q_s.at[h, i], q_r.at[h, i], at.along_zh(step)))
              for i, step in enumerate((2, 1, -1))]
        yield
        for i, step in enumerate((2, 1, -1)):
            ref = rq.at[h, rem4(zh - step)]
            remote(ref, ref, q_s.at[h, i], q_r.at[h, i], at.along_zh(step)).wait_recv()
        fin[h, x] = add(rq[h, 0], rq[h, 1], rq[h, 2], rq[h, 3]).astype(BF)
        for s, step in enumerate((1, -1)):
            go(remote(fin.at[h, x], fin.at[h, x], g_s.at[h, s], g_r.at[h, s], at.along_x(step)))
        yield
        for s, (step, part) in enumerate(((1, low), (-1, high))):
            ref = fin.at[h, rem4(x - step)]
            remote(ref, ref, g_s.at[h, s], g_r.at[h, s], at.along_x(step)).wait_recv()
            ref = fin.at[h, rem4(x - step), part]
            go(remote(ref, ref, gg_s.at[h, s], gg_r.at[h, s], at.along_x(step)))
        yield
        for s, (step, part) in enumerate(((1, low), (-1, high))):
            ref = fin.at[h, rem4(x + 2), part]
            remote(ref, ref, gg_s.at[h, s], gg_r.at[h, s], at.along_x(step)).wait_recv()
        outs = (tot_sq, tot_sk, tot_sv, tot_so) if h == 0 else (tot_tq, tot_tk, tot_tv, tot_to)
        for w in range(3):
            outs[w][...] = fin[h, w].astype(F32)
        wide = fin[h, 3].astype(F32)
        outs[3][:, :640] = wide[:40]
        outs[3][:, 640:] = wide[40:]

    first, second = chain(1), chain(0)
    live = [first]
    step = 0
    while live:
        for c in list(live):
            try:
                next(c)
            except StopIteration:
                live.remove(c)
        step += 1
        if step == 1:
            live.append(second)
            next(second)
        if step == 2:
            for i in range(1, 16):
                ref = rgr.at[lax.rem(me + 16 - i, 16)]
                remote(ref, ref, e_s.at[i], e_r.at[i], at.peer(i)).wait_recv()
            total = rgr[0].astype(F32)
            for i in range(1, 16):
                total = total + rgr[i].astype(F32)
            total = total.astype(BF)
            for wl in wloads:
                wl.wait()
            rg[...] = (dot(total[:, :640], wts[0].reshape(1280, 640), 1, 1)
                       + dot(total[:, 640:], wts[1].reshape(1280, 640), 1, 1)).astype(BF)
    for copy in sends:
        copy.wait_send()


def reduce_all(dws, dwt, gr, full):
    dma = pltpu.SemaphoreType.DMA
    s = jax.ShapeDtypeStruct
    tall, flat = s((80, 640), F32), s((40, 1280), F32)
    v = pltpu.VMEM
    b = (80, 640)
    return pl.pallas_call(
        reduce_kernel,
        out_shape=(tall, tall, tall, flat) * 2 + (s((8, 1280), BF),),
        in_specs=[ANY, ANY, VM, ANY],
        out_specs=(VM,) * 9,
        scratch_shapes=[v((2, 2, 4, 4) + b, BF), v((2, 2, 4, 4) + b, BF), v((2, 2, 4) + b, BF), v((2, 2, 4) + b, BF),
                        v((2, 4) + b, BF), v((2, 2, 4) + b, BF), v((2, 4) + b, BF), v((2,) + b, BF),
                        v((2, 2) + b, BF), v((2, 4) + b, BF), v((2, 4) + b, BF), v((16, 8, 1280), BF),
                        v((2, 16) + b, BF)]
        + [dma((2, 2, 4))] * 3 + [dma((2, 2))] * 4 + [dma((2, 4))] * 2 + [dma((2, 2, 4))] * 2
        + [dma((2, 2))] * 4 + [dma((2, 3))] * 2 + [dma((2, 2))] * 4 + [dma((16,))] * 2 + [dma((2,))],
        compiler_params=pltpu.CompilerParams(collective_id=3, has_side_effects=True, vmem_limit_bytes=60 << 20),
        name="reduce_gradients",
    )(dws, dwt, gr, full)

def position_table(count, width):
    frame_ids = jnp.arange(count, dtype=jnp.int32).astype(F32)
    halves = jnp.arange(width // 2, dtype=jnp.int32).astype(F32)
    rates = jnp.exp(halves * (-2.0 * math.log(10000.0) / width))
    angles = frame_ids[:, None] * rates[None, :]
    return jnp.stack([jnp.sin(angles), jnp.cos(angles)], -1).reshape(count, width)


def per_device(frames_in, ref_feats, out_grad, space_query, space_key, space_value, space_output,
               time_query, time_key, time_value, time_output):
    def narrow(weight):
        return jnp.concatenate([weight[:, :640], weight[:, 640:]], 0)

    pack = jnp.stack([space_query, space_key, space_value, narrow(space_output),
                      time_query, time_key, time_value, narrow(time_output)])
    full, refs = gather(pack, jnp.pad(ref_feats[0], ((0, 2), (0, 0))))
    refs = refs.reshape(128, 1280)
    frames, grads = frames_in.reshape(192, 1280), out_grad.reshape(192, 1280)
    h1, qkv, rkv, o, h1r, ogr = space(frames, refs, grads, full)
    backr, dwt = temporal(h1r, ogr, position_table(32, 1280), full)
    out, frames_grad, dws, gr = back(backr, frames, refs, h1, qkv, rkv, o, full)
    *totals, rg = reduce_all(dws, dwt, gr.reshape(16, 8, 1280), full)
    return (out.reshape(frames_in.shape), frames_grad.reshape(frames_in.shape), rg[None, :6], *totals)


def solution(mesh):
    rows, refs, weight = P("clip", "frame", None, None), P("clip", "frame", None), P("frame", None)
    return jax.shard_map(
        per_device, mesh=mesh, in_specs=(rows, refs, rows) + (weight,) * 8,
        out_specs=(rows, rows, refs) + (weight,) * 8, check_vma=False)
```

```python
import math

import jax
import jax.numpy as jnp
from jax import lax
from jax.experimental import pallas as pl
from jax.experimental.pallas import tpu as pltpu
from jax.sharding import PartitionSpec as P


MESH = pl.DeviceIdType.MESH
ANY = pl.BlockSpec(memory_space=pl.ANY)
VM = pl.BlockSpec(memory_space=pltpu.VMEM)


class Place:
    def __init__(self):
        clip, frame = lax.axis_index("clip"), lax.axis_index("frame")
        self.clip, self.frame = clip, frame
        self.x, self.zh = lax.rem(clip, 4), lax.div(clip, 4)
        self.y, self.zl, self.core = lax.div(frame, 4), lax.rem(lax.div(frame, 2), 2), lax.rem(frame, 2)
        self.parity = lax.rem(self.x, 2)
        self.sibling = (clip, frame + 1 - 2 * self.core)

    def along_y(self, step):
        return (self.clip, lax.rem(self.y + 4 + step, 4) * 4 + self.zl * 2 + self.core)

    def along_x(self, step):
        return (self.zh * 4 + lax.rem(self.x + 4 + step, 4), self.frame)

    def along_z(self, step):
        far = lax.rem(self.zh * 2 + self.zl + 8 + step, 8)
        return (lax.div(far, 2) * 4 + self.x, self.y * 4 + lax.rem(far, 2) * 2 + self.core)

    def along_zh(self, step):
        return (lax.rem(self.zh + 4 + step, 4) * 4 + self.x, self.frame)

    def peer(self, step):
        return (self.clip, lax.rem(self.frame + step, 16))


def greet(devices):
    barrier = pltpu.get_barrier_semaphore()
    for device in devices:
        pl.semaphore_signal(barrier, inc=1, device_id=device, device_id_type=MESH)
    pl.semaphore_wait(barrier, len(devices))


def remote(src, dst, send, recv, device):
    return pltpu.make_async_remote_copy(
        src_ref=src, dst_ref=dst, send_sem=send, recv_sem=recv, device_id=device, device_id_type=MESH)


def shard_of(y, zl, core):
    return lax.rem(y + 8, 4) * 4 + zl * 2 + core


BF, F32 = jnp.bfloat16, jnp.float32
EPSILON = 1e-05
SCALE = 160 ** -0.5


def dot(a, b, ca=1, cb=0):
    return lax.dot_general(a, b, (((ca,), (cb,)), ((), ())), preferred_element_type=F32)


def stats(wide):
    offset = wide - jnp.mean(wide, -1, keepdims=True)
    inverse = lax.rsqrt(jnp.mean(offset * offset, -1, keepdims=True) + EPSILON)
    return offset * inverse, inverse


def stats_back(centred, inverse, g):
    first = jnp.mean(g, -1, keepdims=True)
    second = jnp.mean(g * centred, -1, keepdims=True)
    return inverse * (g - first - centred * second)


def iota(shape, dim):
    return lax.broadcasted_iota(jnp.int32, shape, dim)


def one_hot(hit):
    return jnp.where(hit, 1.0, 0.0).astype(BF)


def frame_pack():
    r, c = iota((256, 192), 0), iota((256, 192), 1)
    d, j = lax.shift_right_logical(r, 4), lax.bitwise_and(r, 15)
    a = jnp.where(j >= 6, 1, 0)
    return one_hot((j < 12) & (c == 90 * a + 6 * d + j))


def frame_unpack():
    c, r = iota((192, 256), 0), iota((192, 256), 1)
    d, j = lax.shift_right_logical(r, 4), lax.bitwise_and(r, 15)
    a = jnp.where(j >= 6, 1, 0)
    return one_hot((j < 12) & (c == 90 * a + 6 * d + j))


def token_unpack():
    m, r = iota((192, 256), 0), iota((192, 256), 1)
    t, f, a = lax.shift_right_logical(m, 5), lax.bitwise_and(lax.shift_right_logical(m, 1), 15), lax.bitwise_and(m, 1)
    return one_hot(r == 16 * f + 6 * a + t)


def token_pack():
    m, r = iota((256, 192), 1), iota((256, 192), 0)
    t, f, a = lax.shift_right_logical(m, 5), lax.bitwise_and(lax.shift_right_logical(m, 1), 15), lax.bitwise_and(m, 1)
    return one_hot(r == 16 * f + 6 * a + t)


def ref_unpack(rows, cols, swap=False):
    m, r = (iota((rows, cols), 0), iota((rows, cols), 1)) if not swap else (iota((rows, cols), 1), iota((rows, cols), 0))
    d, j = lax.shift_right_logical(r, 3), lax.bitwise_and(r, 7)
    return one_hot((j < 6) & (m == 6 * d + j))


def head_masks():
    lane = iota((1, 640), 1)
    return [(lane >= 160 * h) & (lane < 160 * (h + 1)) for h in range(4)]


def stack_heads(rows, masks):
    return jnp.concatenate([rows * one_hot(m) for m in masks], 0)


def merge_heads(stacked, masks):
    n = stacked.shape[0] // 4
    total = jnp.where(masks[0], stacked[:n], 0.0)
    for h in range(1, 4):
        total = jnp.where(masks[h], stacked[h * n:(h + 1) * n], total)
    return total


def softmax(stacked, keys, same=None):
    powers = jnp.exp(dot(stacked, keys, 1, 1) * SCALE)
    if same is not None:
        powers = jnp.where(same, powers, 0.0)
    return powers / jnp.sum(powers, -1, keepdims=True)


def score_back(probs, grads, values):
    dp = dot(grads, values, 1, 1)
    return (probs * (dp - jnp.sum(probs * dp, -1, keepdims=True)) * SCALE).astype(BF)


def wide_output(slot):
    wide = slot.astype(F32)
    left = wide[:, :40].reshape(640, 640).astype(BF)
    right = wide[:, 40:].reshape(640, 640).astype(BF)
    return left, right


def pack_output(left, right):
    return jnp.concatenate([left.reshape(16, 40, 640), right.reshape(16, 40, 640)], 1)


def store_term(dw, w, term):
    parts = term.reshape(4, 2, 2, 80, 640).astype(BF)
    for core in range(2):
        for zl in range(2):
            dw[core, zl, w] = parts[:, zl, core]


def exchange_start(at, src, dst, send, recv):
    copies = []
    for i in range(1, 16):
        to = lax.rem(at.frame + i, 16)
        copy = remote(src.at[pl.ds(pl.multiple_of(16 * to, 16), 16)],
                      dst.at[pl.ds(pl.multiple_of(16 * at.frame, 16), 16)], send.at[i], recv.at[i], at.peer(i))
        copy.start()
        copies.append(copy)
    own = pl.ds(pl.multiple_of(16 * at.frame, 16), 16)
    dst[own, :] = src[own, :]
    return copies


def load(src, dst, sem):
    copy = pltpu.make_async_copy(src, dst, sem)
    copy.start()
    return copy


def time_kernel(h1r, ogr, table, full, back, dw, wts, buf, wsem, s_s, r_s):
    at = Place()
    loads = [load(full.at[:, i], wts.at[i], wsem.at[i]) for i in range(4)]
    greet([at.peer(i) for i in range(1, 16)])
    masks = head_masks()
    unpack = token_unpack()
    h1 = dot(unpack, h1r[...])
    og = dot(unpack, ogr[...]).astype(BF)
    centred, inverse = stats(h1)
    n2 = (centred + jnp.concatenate([table[...]] * 6, 0)).astype(BF)
    parts = []
    for i in range(3):
        loads[i].wait()
        parts.append(dot(n2, wts[i].reshape(1280, 640)).astype(BF))
    q, k, v = parts
    r, c = iota((768, 192), 0), iota((768, 192), 1)
    r = jnp.where(r >= 384, r - 384, r)
    r = jnp.where(r >= 192, r - 192, r)
    same = lax.shift_right_logical(r, 5) == lax.shift_right_logical(c, 5)
    qs = stack_heads(q, masks)
    probs = softmax(qs, k, same)
    pb = probs.astype(BF)
    o2 = merge_heads(dot(pb, v), masks).astype(BF)
    loads[3].wait()
    left, right = wide_output(wts[3])
    go = (dot(og[:, :640], left, 1, 1) + dot(og[:, 640:], right, 1, 1)).astype(BF)
    gs = stack_heads(go, masks)
    eb = score_back(probs, gs, v)
    gq = merge_heads(dot(eb, k), masks).astype(BF)
    gk = dot(eb, qs, 0, 0).astype(BF)
    gv = dot(pb, gs, 0, 0).astype(BF)
    grads = (gq, gk, gv)
    gn = dot(gq, wts[0].reshape(1280, 640), 1, 1)
    for i in (1, 2):
        gn = gn + dot(grads[i], wts[i].reshape(1280, 640), 1, 1)
    gh = (og.astype(F32) + stats_back(centred, inverse, gn)).astype(BF)
    pack = token_pack()
    buf[:, :1280] = dot(pack, gh).astype(BF)
    buf[:, 1280:] = dot(pack, o2).astype(BF)
    copies = exchange_start(at, buf, back, s_s, r_s)
    for i in range(3):
        store_term(dw, i, dot(n2, grads[i], 0, 0))
    store_term(dw, 3, pack_output(dot(o2, og[:, :640], 0, 0), dot(o2, og[:, 640:], 0, 0)))
    for copy in copies:
        copy.wait()


def temporal(h1r, ogr, table, full):
    dma = pltpu.SemaphoreType.DMA
    s = jax.ShapeDtypeStruct
    return pl.pallas_call(
        time_kernel,
        out_shape=(s((256, 1920), BF), s((2, 2, 4, 4, 80, 640), BF)),
        in_specs=[VM, VM, VM, ANY],
        out_specs=(VM, VM),
        scratch_shapes=[pltpu.VMEM((4, 16, 80, 640), BF), pltpu.VMEM((256, 1920), BF),
                        dma((4,)), dma((16,)), dma((16,))],
        compiler_params=pltpu.CompilerParams(collective_id=2, has_side_effects=True, vmem_limit_bytes=60 << 20),
        name="time_both",
    )(h1r, ogr, table, full)


def first_kernel(frames, ref_in, og, w0, w1, w2, w3, w4, w5, w6, w7,
                 h1_o, qkv_o, rkv_o, o_o, h1r, ogr, refs, full_so, full_t,
                 pack, ref8, full_s, buf_a, buf_b, sib_s, sib_r, y_s, y_r, rel_s, rel_r, z_s, z_r, x_s, x_r,
                 ref_s, ref_r, s_s, r_s, loc):
    at = Place()
    y, zl, core, p, me = at.y, at.zl, at.core, at.parity, at.frame
    for i, w in enumerate((w0, w1, w2, None, w4, w5, w6)):
        if w is not None:
            pack[i] = w[...]
    for i, w in ((3, w3), (7, w7)):
        wide = w[...].astype(F32)
        pack[i] = jnp.concatenate([wide[:, :640], wide[:, 640:]], 0).astype(BF)
    small = ref_in[...].astype(F32)
    ref8[...] = jnp.concatenate([small, small[:2] * 0.0], 0).astype(BF)
    greet([at.along_x(1), at.along_x(-1), at.along_z(1), at.along_z(-1)] + [at.peer(i) for i in range(1, 16)])
    sends = []

    def go(copy):
        copy.start()
        sends.append(copy)

    steps = (1, -1)
    fulls = (full_s, full_t)
    keeps = []

    def chain(h):
        full = fulls[h]
        rows = [shard_of(y + k, zl, core) for k in range(4)]
        over = [shard_of(y + k, 1 - zl, core) for k in range(4)]

        def pair(j):
            return pl.ds(2 * j, 2)

        def to_sibling(index, ref):
            go(remote(ref, ref, sib_s.at[h, index], sib_r.at[h, index], at.sibling))

        def z_send(k, src=None):
            for d in range(2):
                w = 2 * p + d
                dst = full.at[rows[k], w]
                go(remote(dst if src is None else src.at[4 * h + w], dst, z_s.at[h, k, d], z_r.at[h, k, d],
                          at.along_z(1 - 2 * d)))

        def z_wait(k):
            for d in range(2):
                ref = full.at[over[k], 2 * p + d]
                remote(ref, ref, z_s.at[h, k, d], z_r.at[h, k, d], at.along_z(1)).wait_recv()
                go(remote(ref, ref, x_s.at[h, k, d], x_r.at[h, k, d], at.along_x(1 - 2 * d)))
                to_sibling(7 + 2 * k + d, ref)

        def x_wait(k):
            for d in range(2):
                ref = full.at[over[k], 2 * (1 - p) + d]
                remote(ref, ref, x_s.at[h, k, d], x_r.at[h, k, d], at.along_x(1)).wait_recv()
                to_sibling(15 + 2 * k + d, ref)

        half = pl.ds(4 * h, 4)
        for j in range(2):
            for s, step in enumerate(steps):
                go(remote(pack.at[pl.ds(4 * h + 2 * j, 2)], full.at[me, pair(j)], y_s.at[h, s, j], y_r.at[h, s, j],
                          at.along_y(step)))
        z_send(0, pack)
        go(remote(pack.at[half], full.at[me], sib_s.at[h, 0], sib_r.at[h, 0], at.sibling))
        keeps.append(load(pack.at[half], full.at[me], loc.at[h]))
        yield
        for j in range(2):
            for s, step in enumerate(steps):
                ref = full.at[rows[(4 - step) % 4], pair(j)]
                remote(ref, ref, y_s.at[h, s, j], y_r.at[h, s, j], at.along_y(step)).wait_recv()
                if j == s:
                    go(remote(ref, ref, rel_s.at[h, j], rel_r.at[h, j], at.along_y(step)))
                to_sibling(1 + 2 * s + j, ref)
        z_send(1)
        z_send(3)
        yield
        z_wait(0)
        for j in range(2):
            ref = full.at[rows[2], pair(j)]
            remote(ref, ref, rel_s.at[h, j], rel_r.at[h, j], at.along_y(1)).wait_recv()
            to_sibling(5 + j, ref)
        z_send(2)
        yield
        z_wait(1)
        z_wait(3)
        x_wait(0)
        yield
        z_wait(2)
        x_wait(1)
        x_wait(3)
        yield
        x_wait(2)
        yield

        def sib_wait(index, ref):
            remote(ref, ref, sib_s.at[h, index], sib_r.at[h, index], at.sibling).wait_recv()

        other = [shard_of(y + k, zl, 1 - core) for k in range(4)]
        sib_wait(0, full.at[other[0]])
        for s, step in enumerate(steps):
            for j in range(2):
                sib_wait(1 + 2 * s + j, full.at[other[(4 - step) % 4], pair(j)])
        for j in range(2):
            sib_wait(5 + j, full.at[other[2], pair(j)])
        for k in range(4):
            for d in range(2):
                far = shard_of(y + k, 1 - zl, 1 - core)
                sib_wait(7 + 2 * k + d, full.at[far, 2 * p + d])
                sib_wait(15 + 2 * k + d, full.at[far, 2 * (1 - p) + d])

    now, later = chain(0), chain(1)
    next(now)
    for i in range(1, 16):
        go(remote(ref8, refs.at[me], ref_s.at[i], ref_r.at[i], at.peer(i)))
    refs[me] = ref8[...]
    pack_rows = frame_pack()
    buf_a[...] = dot(pack_rows, og[...]).astype(BF)
    masks = head_masks()
    wide = frames[...].astype(F32)
    n1 = stats(wide)[0].astype(BF)
    next(now)
    next(now)
    next(later)
    next(now)
    next(now)
    next(now)
    for i in range(1, 16):
        ref = refs.at[lax.rem(me + 16 - i, 16)]
        remote(ref, ref, ref_s.at[i], ref_r.at[i], at.peer(i)).wait_recv()
    for _ in now:
        pass
    keeps[0].wait()
    keep = load(full_s, full_so, loc.at[2])
    copies = exchange_start(at, buf_a, ogr, s_s.at[0], r_s.at[0])
    ref = dot(ref_unpack(96, 128), refs[...].astype(F32).reshape(128, 1280).astype(BF)).astype(BF)
    q = dot(n1, full_s[:, 0].reshape(1280, 640)).astype(BF)
    w = full_s[:, 1].reshape(1280, 640)
    k, rk = dot(n1, w).astype(BF), dot(ref, w).astype(BF)
    next(later)
    w = full_s[:, 2].reshape(1280, 640)
    v, rv = dot(n1, w).astype(BF), dot(ref, w).astype(BF)
    for i, part in enumerate((q, k, v)):
        qkv_o[i] = part
    rkv_o[0] = rk
    rkv_o[1] = rv
    outs = []
    for a in range(2):
        rows = slice(96 * a, 96 * a + 96)
        keys = jnp.concatenate([k[rows], rk], 0)
        values = jnp.concatenate([v[rows], rv], 0)
        probs = softmax(stack_heads(q[rows], masks), keys).astype(BF)
        outs.append(merge_heads(dot(probs, values), masks))
        next(later)
    o = jnp.concatenate(outs, 0).astype(BF)
    o_o[...] = o
    left, right = wide_output(full_s[:, 3])
    h1 = (wide + jnp.concatenate([dot(o, left), dot(o, right)], 1)).astype(BF)
    h1_o[...] = h1
    buf_b[...] = dot(pack_rows, h1).astype(BF)
    copies += exchange_start(at, buf_b, h1r, s_s.at[1], r_s.at[1])
    for _ in later:
        pass
    for copy in copies:
        copy.wait()
    for copy in sends:
        copy.wait_send()
    keep.wait()
    keeps[1].wait()


def first(frames, ref_in, og, weights):
    dma = pltpu.SemaphoreType.DMA
    s = jax.ShapeDtypeStruct
    v = pltpu.VMEM
    return pl.pallas_call(
        first_kernel,
        out_shape=(s((192, 1280), BF), s((3, 192, 640), BF), s((2, 96, 640), BF), s((192, 640), BF),
                   s((256, 1280), BF), s((256, 1280), BF), s((16, 8, 1280), BF), s((16, 4, 80, 640), BF),
                   s((16, 4, 80, 640), BF)),
        in_specs=[VM] * 11,
        out_specs=(VM,) * 7 + (ANY, ANY),
        scratch_shapes=[v((8, 80, 640), BF), v((8, 1280), BF), v((16, 4, 80, 640), BF), v((256, 1280), BF),
                        v((256, 1280), BF), dma((2, 23)), dma((2, 23)), dma((2, 2, 2)), dma((2, 2, 2)), dma((2, 2)),
                        dma((2, 2)), dma((2, 4, 2)), dma((2, 4, 2)), dma((2, 4, 2)), dma((2, 4, 2)), dma((16,)),
                        dma((16,)), dma((2, 16)), dma((2, 16)), dma((3,))],
        compiler_params=pltpu.CompilerParams(collective_id=0, has_side_effects=True, vmem_limit_bytes=60 << 20),
        name="gather_and_space_forward",
    )(frames, ref_in, og, *weights)


def add(*parts):
    total = parts[0].astype(F32)
    for part in parts[1:]:
        total = total + part.astype(F32)
    return total


def last_kernel(backr, frames, refs, h1, qkv, rkv, o_in, full_s, full_t, dwt,
                out_o, fg_o, rg, fin,
                wts, dws, gt, r0, rx, rz, ry1, ry2, pm, rax1, rax2, rq, gr, rgr,
                wsem, l_m, c_s, c_r, x_s, x_r, z_s, z_r, y1_s, y1_r, y2_s, y2_r,
                a1_s, a1_r, a2_s, a2_r, q_s, q_r, qq_s, qq_r, g_s, g_r, gg_s, gg_r, e_s, e_r):
    at = Place()
    y, zl, p, x, zh, me = at.y, at.zl, at.parity, at.x, at.zh, at.frame
    core, oz = at.core, 1 - at.zl
    loads = {7: load(full_t.at[:, 3], wts.at[0], wsem.at[0])}
    for n, i in enumerate((3, 0, 1, 2)):
        loads[i] = load(full_s.at[:, i], wts.at[1 + n], wsem.at[1 + n])
    mine = {}
    for a, zz in enumerate((oz, zl)):
        for w in range(4):
            mine[a, w] = load(dwt.at[core, zz, w], gt.at[zz, w], l_m.at[a, w])
    greet([at.peer(i) for i in range(1, 16)] + [at.along_x(1), at.along_x(-1), at.along_z(1), at.along_z(-1),
                                                at.along_zh(1), at.along_zh(-1)])
    sends = []

    def go(copy):
        copy.start()
        sends.append(copy)
        return copy

    def rem4(v):
        return lax.rem(v + 8, 4)

    cross = {}

    def send_cross(h, w):
        src = dws if h == 0 else dwt
        for a, zz in enumerate((oz, zl)):
            cross[h, a, w] = go(remote(src.at[1 - core, zz, w], r0.at[h, a, w], c_s.at[h, a, w], c_r.at[h, a, w],
                                       at.sibling))

    def chain(h):
        g = dws.at[core] if h == 0 else gt
        low, high = pl.ds(0, 48), pl.ds(48, 32)
        ys = [rem4(y + k) for k in range(4)]
        xc, zc = {}, {}

        def take(a, zz):
            for w in range(4):
                if h == 1:
                    mine[a, w].wait()
                cross[h, a, w].wait_recv()
                g[zz, w] = add(g[zz, w], r0[h, a, w]).astype(BF)

        def x_take(k):
            for d in range(2):
                xc[k, d].wait_recv()
                w = 2 * p + d
                g[oz, w, ys[k]] = add(g[oz, w, ys[k]], rx[h, d, k]).astype(BF)
                zc[k, d] = go(remote(g.at[oz, w, ys[k]], rz.at[h, d, k], z_s.at[h, d, k], z_r.at[h, d, k],
                                     at.along_z(2 * d - 1)))

        def z_take(k):
            for d in range(2):
                zc[k, d].wait_recv()
                w = 2 * p + d
                g[zl, w, ys[k]] = add(g[zl, w, ys[k]], rz[h, d, k]).astype(BF)

        take(0, oz)
        for k in (2, 1, 3, 0):
            for d in range(2):
                xc[k, d] = go(remote(g.at[oz, 2 * (1 - p) + d, ys[k]], rx.at[h, d, k], x_s.at[h, d, k],
                                     x_r.at[h, d, k], at.along_x(2 * d - 1)))
        take(1, zl)
        yield
        x_take(2)
        x_take(1)
        yield
        z_take(2)
        y1 = [go(remote(g.at[zl, w, ys[2]], ry1.at[h, w], y1_s.at[h, w], y1_r.at[h, w],
                        at.along_y(-1 if w < 2 else 1))) for w in range(4)]
        x_take(3)
        yield
        x_take(0)
        z_take(1)
        z_take(3)
        yield
        y2 = {}
        for w in (0, 2, 1, 3):
            y1[w].wait_recv()
            on = ys[3 if w < 2 else 1]
            g[zl, w, on] = add(g[zl, w, on], ry1[h, w]).astype(BF)
            for s, step in enumerate((1, -1)):
                y2[s, w] = go(remote(g.at[zl, w, ys[step % 4]], ry2.at[s, h, w], y2_s.at[s, h, w],
                                     y2_r.at[s, h, w], at.along_y(step)))
        z_take(0)
        yield
        for w in (0, 2, 1, 3):
            y2[0, w].wait_recv()
            y2[1, w].wait_recv()
            pm[h, w] = add(g[zl, w, y], ry2[0, h, w], ry2[1, h, w]).astype(BF)
        far = rem4(x + 2)
        a1 = [go(remote(pm.at[h, far, part], rax1.at[h, part], a1_s.at[h, s], a1_r.at[h, s], at.along_x(step)))
              for s, (step, part) in enumerate(((1, low), (-1, high)))]
        yield
        for s, (step, part) in enumerate(((1, low), (-1, high))):
            a1[s].wait_recv()
            on = rem4(x + step)
            pm[h, on, part] = add(pm[h, on, part], rax1[h, part]).astype(BF)
        a2 = [go(remote(pm.at[h, rem4(x + step)], rax2.at[s, h], a2_s.at[s, h], a2_r.at[s, h], at.along_x(step)))
              for s, step in enumerate((1, -1))]
        yield
        for copy in a2:
            copy.wait_recv()
        rq[h, zh] = add(pm[h, x], rax2[0, h], rax2[1, h]).astype(BF)
        for s, step in enumerate((1, -1)):
            go(remote(rq.at[h, zh], rq.at[h, zh], q_s.at[h, s], q_r.at[h, s], at.along_zh(step)))
        yield
        for s, (step, part) in enumerate(((1, low), (-1, high))):
            ref = rq.at[h, rem4(zh - step)]
            remote(ref, ref, q_s.at[h, s], q_r.at[h, s], at.along_zh(step)).wait_recv()
            ref = rq.at[h, rem4(zh - step), part]
            go(remote(ref, ref, qq_s.at[h, s], qq_r.at[h, s], at.along_zh(step)))
        yield
        for s, (step, part) in enumerate(((1, low), (-1, high))):
            ref = rq.at[h, rem4(zh + 2), part]
            remote(ref, ref, qq_s.at[h, s], qq_r.at[h, s], at.along_zh(step)).wait_recv()
        fin[h, x] = add(rq[h, 0], rq[h, 1], rq[h, 2], rq[h, 3]).astype(BF)
        for s, step in enumerate((1, -1)):
            go(remote(fin.at[h, x], fin.at[h, x], g_s.at[h, s], g_r.at[h, s], at.along_x(step)))
        yield
        for s, (step, part) in enumerate(((1, low), (-1, high))):
            ref = fin.at[h, rem4(x - step)]
            remote(ref, ref, g_s.at[h, s], g_r.at[h, s], at.along_x(step)).wait_recv()
            ref = fin.at[h, rem4(x - step), part]
            go(remote(ref, ref, gg_s.at[h, s], gg_r.at[h, s], at.along_x(step)))
        yield
        for s, (step, part) in enumerate(((1, low), (-1, high))):
            ref = fin.at[h, rem4(x + 2), part]
            remote(ref, ref, gg_s.at[h, s], gg_r.at[h, s], at.along_x(step)).wait_recv()

    for w in range(4):
        send_cross(1, w)
    early = chain(1)
    masks = head_masks()
    unpack = frame_unpack()
    gh = dot(unpack, backr[:, :1280]).astype(BF)
    o2 = dot(unpack, backr[:, 1280:]).astype(BF)
    next(early)
    loads[3].wait()
    left, right = wide_output(wts[1])
    go_ = (dot(gh[:, :640], left, 1, 1) + dot(gh[:, 640:], right, 1, 1)).astype(BF)
    rk, rv = rkv[0], rkv[1]
    gq, gk, gv = [], [], []
    grk = grv = None
    for a in range(2):
        rows = slice(96 * a, 96 * a + 96)
        keys = jnp.concatenate([qkv[1, rows], rk], 0)
        values = jnp.concatenate([qkv[2, rows], rv], 0)
        qs = stack_heads(qkv[0, rows], masks)
        gs = stack_heads(go_[rows], masks)
        probs = softmax(qs, keys)
        eb = score_back(probs, gs, values)
        gq.append(merge_heads(dot(eb, keys), masks))
        gkeys = dot(eb, qs, 0, 0)
        gvalues = dot(probs.astype(BF), gs, 0, 0)
        gk.append(gkeys[:96])
        gv.append(gvalues[:96])
        grk = gkeys[96:] if grk is None else grk + gkeys[96:]
        grv = gvalues[96:] if grv is None else grv + gvalues[96:]
        next(early)
    gq, gk, gv = (jnp.concatenate(g, 0).astype(BF) for g in (gq, gk, gv))
    grk, grv = grk.astype(BF), grv.astype(BF)
    centred, inverse = stats(frames[...].astype(F32))
    n1 = centred.astype(BF)
    ref = dot(ref_unpack(96, 128), refs[...]).astype(BF)
    o = o_in[...]
    store_term(dws, 3, pack_output(dot(o, gh[:, :640], 0, 0), dot(o, gh[:, 640:], 0, 0)))
    send_cross(0, 3)
    store_term(dws, 0, dot(n1, gq, 0, 0))
    send_cross(0, 0)
    store_term(dws, 1, dot(n1, gk, 0, 0) + dot(ref, grk, 0, 0))
    send_cross(0, 1)
    store_term(dws, 2, dot(n1, gv, 0, 0) + dot(ref, grv, 0, 0))
    send_cross(0, 2)
    spread = ref_unpack(128, 96, True)
    gr[:, :, :640] = dot(spread, grk).reshape(16, 8, 640).astype(BF)
    gr[:, :, 640:] = dot(spread, grv).reshape(16, 8, 640).astype(BF)
    rgr[me] = gr[me]
    late = chain(0)
    next(early)
    next(late)
    for i in range(1, 16):
        to = lax.rem(me + i, 16)
        go(remote(gr.at[to], rgr.at[me], e_s.at[i], e_r.at[i], at.peer(i)))

    def finish_rows():
        gn = None
        for n, (i, g) in enumerate(((0, gq), (1, gk), (2, gv))):
            loads[i].wait()
            term = dot(g, wts[2 + n].reshape(1280, 640), 1, 1)
            gn = term if gn is None else gn + term
        fg_o[...] = (gh.astype(F32) + stats_back(centred, inverse, gn)).astype(BF)

    def finish_out():
        loads[7].wait()
        left, right = wide_output(wts[0])
        out_o[...] = (h1[...].astype(F32) + jnp.concatenate([dot(o2, left), dot(o2, right)], 1)).astype(BF)

    def finish_ref():
        for i in range(1, 16):
            ref = rgr.at[lax.rem(me + 16 - i, 16)]
            remote(ref, ref, e_s.at[i], e_r.at[i], at.peer(i)).wait_recv()
        total = rgr[0].astype(F32)
        for i in range(1, 16):
            total = total + rgr[i].astype(F32)
        total = total.astype(BF)
        rg[...] = (dot(total[:, :640], wts[3].reshape(1280, 640), 1, 1)
                   + dot(total[:, 640:], wts[4].reshape(1280, 640), 1, 1)).astype(BF)

    work = [finish_rows, finish_out, finish_ref]
    live = [early, late]
    while live:
        if work:
            work.pop(0)()
        for c in list(live):
            try:
                next(c)
            except StopIteration:
                live.remove(c)
    for copy in sends:
        copy.wait_send()


def last(backr, frames, refs, h1, qkv, rkv, o, full_s, full_t, dwt):
    dma = pltpu.SemaphoreType.DMA
    s = jax.ShapeDtypeStruct
    v = pltpu.VMEM
    b = (80, 640)
    return pl.pallas_call(
        last_kernel,
        out_shape=(s((192, 1280), BF), s((192, 1280), BF), s((8, 1280), BF), s((2, 4) + b, BF)),
        in_specs=[VM] * 7 + [ANY] * 3,
        out_specs=(VM,) * 4,
        scratch_shapes=[v((5, 16) + b, BF), v((2, 2, 4, 4) + b, BF), v((2, 4, 4) + b, BF), v((2, 2, 4, 4) + b, BF),
                        v((2, 2, 4) + b, BF), v((2, 2, 4) + b, BF), v((2, 4) + b, BF), v((2, 2, 4) + b, BF),
                        v((2, 4) + b, BF), v((2,) + b, BF), v((2, 2) + b, BF), v((2, 4) + b, BF),
                        v((16, 8, 1280), BF), v((16, 8, 1280), BF),
                        dma((5,)), dma((2, 4)), dma((2, 2, 4)), dma((2, 2, 4))]
        + [dma((2, 2, 4))] * 4 + [dma((2, 4))] * 2 + [dma((2, 2, 4))] * 2 + [dma((2, 2))] * 12 + [dma((16,))] * 2,
        compiler_params=pltpu.CompilerParams(collective_id=3, has_side_effects=True, vmem_limit_bytes=62 << 20),
        name="space_backward_and_reduce",
    )(backr, frames, refs, h1, qkv, rkv, o, full_s, full_t, dwt)


def finish_kernel(out, fg, rg, fin, out_o, fg_o, rg_o, *totals):
    out_o[...] = out[...]
    fg_o[...] = fg[...]
    rg_o[...] = rg[...].astype(F32)[:6].astype(BF)
    for h in range(2):
        for w in range(3):
            totals[4 * h + w][...] = fin[h, w].astype(F32)
        wide = fin[h, 3].astype(F32)
        totals[4 * h + 3][:, :640] = wide[:40]
        totals[4 * h + 3][:, 640:] = wide[40:]


def finish(out, fg, rg, fin):
    s = jax.ShapeDtypeStruct
    tall, flat = s((80, 640), F32), s((40, 1280), F32)
    return pl.pallas_call(
        finish_kernel,
        out_shape=(s((192, 1280), BF), s((192, 1280), BF), s((6, 1280), BF)) + (tall, tall, tall, flat) * 2,
        in_specs=[VM] * 4, out_specs=(VM,) * 11, name="write_outputs",
    )(out, fg, rg, fin)

def position_table(count, width):
    column = lax.broadcasted_iota(jnp.int32, (count, width), 1)
    frame = lax.broadcasted_iota(jnp.int32, (count, width), 0).astype(F32)
    rates = jnp.exp((column // 2).astype(F32) * (-2.0 * math.log(10000.0) / width))
    angles = frame * rates
    return jnp.where(column % 2 == 0, jnp.sin(angles), jnp.cos(angles))


def per_device(frames_in, ref_feats, out_grad, *weights):
    frames, grads = frames_in.reshape(192, 1280), out_grad.reshape(192, 1280)
    h1, qkv, rkv, o, h1r, ogr, refs, full_s, full_t = first(frames, ref_feats[0], grads, weights)
    backr, dwt = temporal(h1r, ogr, position_table(32, 1280), full_t)
    results = last(backr, frames, refs.reshape(128, 1280), h1, qkv, rkv, o, full_s, full_t, dwt)
    out, frames_grad, rg, *totals = finish(*results)
    return (out.reshape(frames_in.shape), frames_grad.reshape(frames_in.shape), rg[None], *totals)


def solution(mesh):
    rows, refs, weight = P("clip", "frame", None, None), P("clip", "frame", None), P("frame", None)
    return jax.shard_map(
        per_device, mesh=mesh, in_specs=(rows, refs, rows) + (weight,) * 8,
        out_specs=(rows, rows, refs) + (weight,) * 8, check_vma=False)
```

```python
import math

import jax
import jax.numpy as jnp
from jax import lax
from jax.experimental import pallas as pl
from jax.experimental.pallas import tpu as pltpu
from jax.sharding import PartitionSpec as P


MESH = pl.DeviceIdType.MESH
ANY = pl.BlockSpec(memory_space=pl.ANY)
VM = pl.BlockSpec(memory_space=pltpu.VMEM)


class Place:
    def __init__(self):
        clip, frame = lax.axis_index("clip"), lax.axis_index("frame")
        self.clip, self.frame = clip, frame
        self.x, self.zh = lax.rem(clip, 4), lax.div(clip, 4)
        self.y, self.zl, self.core = lax.div(frame, 4), lax.rem(lax.div(frame, 2), 2), lax.rem(frame, 2)
        self.parity = lax.rem(self.x, 2)
        self.sibling = (clip, frame + 1 - 2 * self.core)

    def along_y(self, step):
        return (self.clip, lax.rem(self.y + 4 + step, 4) * 4 + self.zl * 2 + self.core)

    def along_x(self, step):
        return (self.zh * 4 + lax.rem(self.x + 4 + step, 4), self.frame)

    def along_z(self, step):
        far = lax.rem(self.zh * 2 + self.zl + 8 + step, 8)
        return (lax.div(far, 2) * 4 + self.x, self.y * 4 + lax.rem(far, 2) * 2 + self.core)

    def along_zh(self, step):
        return (lax.rem(self.zh + 4 + step, 4) * 4 + self.x, self.frame)

    def peer(self, step):
        return (self.clip, lax.rem(self.frame + step, 16))


def greet(devices):
    barrier = pltpu.get_barrier_semaphore()
    for device in devices:
        pl.semaphore_signal(barrier, inc=1, device_id=device, device_id_type=MESH)
    pl.semaphore_wait(barrier, len(devices))


def remote(src, dst, send, recv, device):
    return pltpu.make_async_remote_copy(
        src_ref=src, dst_ref=dst, send_sem=send, recv_sem=recv, device_id=device, device_id_type=MESH)


def shard_of(y, zl, core):
    return lax.rem(y + 8, 4) * 4 + zl * 2 + core


BF, F32 = jnp.bfloat16, jnp.float32
EPSILON = 1e-05
SCALE = 160 ** -0.5


def dot(a, b, ca=1, cb=0):
    return lax.dot_general(a, b, (((ca,), (cb,)), ((), ())), preferred_element_type=F32)


def stats(wide):
    offset = wide - jnp.mean(wide, -1, keepdims=True)
    inverse = lax.rsqrt(jnp.mean(offset * offset, -1, keepdims=True) + EPSILON)
    return offset * inverse, inverse


def stats_back(centred, inverse, g):
    first = jnp.mean(g, -1, keepdims=True)
    second = jnp.mean(g * centred, -1, keepdims=True)
    return inverse * (g - first - centred * second)


def iota(shape, dim):
    return lax.broadcasted_iota(jnp.int32, shape, dim)


def one_hot(hit):
    return jnp.where(hit, 1.0, 0.0).astype(BF)


def frame_pack():
    r, c = iota((256, 192), 0), iota((256, 192), 1)
    d, j = lax.shift_right_logical(r, 4), lax.bitwise_and(r, 15)
    a = jnp.where(j >= 6, 1, 0)
    return one_hot((j < 12) & (c == 90 * a + 6 * d + j))


def frame_unpack():
    c, r = iota((192, 256), 0), iota((192, 256), 1)
    d, j = lax.shift_right_logical(r, 4), lax.bitwise_and(r, 15)
    a = jnp.where(j >= 6, 1, 0)
    return one_hot((j < 12) & (c == 90 * a + 6 * d + j))


def token_unpack():
    m, r = iota((192, 256), 0), iota((192, 256), 1)
    t, f, a = lax.shift_right_logical(m, 5), lax.bitwise_and(lax.shift_right_logical(m, 1), 15), lax.bitwise_and(m, 1)
    return one_hot(r == 16 * f + 6 * a + t)


def token_pack():
    m, r = iota((256, 192), 1), iota((256, 192), 0)
    t, f, a = lax.shift_right_logical(m, 5), lax.bitwise_and(lax.shift_right_logical(m, 1), 15), lax.bitwise_and(m, 1)
    return one_hot(r == 16 * f + 6 * a + t)


def ref_unpack(rows, cols, swap=False):
    m, r = (iota((rows, cols), 0), iota((rows, cols), 1)) if not swap else (iota((rows, cols), 1), iota((rows, cols), 0))
    d, j = lax.shift_right_logical(r, 3), lax.bitwise_and(r, 7)
    return one_hot((j < 6) & (m == 6 * d + j))


def head_masks():
    lane = iota((1, 640), 1)
    return [(lane >= 160 * h) & (lane < 160 * (h + 1)) for h in range(4)]


def stack_heads(rows, masks):
    return jnp.concatenate([rows * one_hot(m) for m in masks], 0)


def merge_heads(stacked, masks):
    n = stacked.shape[0] // 4
    total = jnp.where(masks[0], stacked[:n], 0.0)
    for h in range(1, 4):
        total = jnp.where(masks[h], stacked[h * n:(h + 1) * n], total)
    return total


def softmax(stacked, keys, same=None):
    powers = jnp.exp(dot(stacked, keys, 1, 1) * SCALE)
    if same is not None:
        powers = jnp.where(same, powers, 0.0)
    return powers / jnp.sum(powers, -1, keepdims=True)


def score_back(probs, grads, values):
    dp = dot(grads, values, 1, 1)
    return (probs * (dp - jnp.sum(probs * dp, -1, keepdims=True)) * SCALE).astype(BF)


def wide_output(slot):
    wide = slot.astype(F32)
    left = wide[:, :40].reshape(640, 640).astype(BF)
    right = wide[:, 40:].reshape(640, 640).astype(BF)
    return left, right


def pack_output(left, right):
    return jnp.concatenate([left.reshape(16, 40, 640), right.reshape(16, 40, 640)], 1)


def store_term(dw, w, term):
    parts = term.reshape(4, 2, 2, 80, 640).astype(BF)
    for core in range(2):
        for zl in range(2):
            dw[core, zl, w] = parts[:, zl, core]


def exchange_start(at, src, dst, send, recv):
    copies = []
    for i in range(1, 16):
        to = lax.rem(at.frame + i, 16)
        copy = remote(src.at[pl.ds(pl.multiple_of(16 * to, 16), 16)],
                      dst.at[pl.ds(pl.multiple_of(16 * at.frame, 16), 16)], send.at[i], recv.at[i], at.peer(i))
        copy.start()
        copies.append(copy)
    own = pl.ds(pl.multiple_of(16 * at.frame, 16), 16)
    dst[own, :] = src[own, :]
    return copies


def load(src, dst, sem):
    copy = pltpu.make_async_copy(src, dst, sem)
    copy.start()
    return copy


def add(*parts):
    total = parts[0].astype(F32)
    for part in parts[1:]:
        total = total + part.astype(F32)
    return total


def whole_kernel(frames, ref_in, og_in, table, w0, w1, w2, w3, w4, w5, w6, w7,
                 out_o, fg_o, rg, fin,
                 pack, ref8, full_s, full_t, refs, qkv, rkv, o_in, h1_in,
                 buf_b, h1r, buf_g, ogr, buf_o, o2r, buf, backr,
                 dws, dwt, r0, rx, rz, ry1, ry2, pm, rax1, rax2, rq, gr, rgr,
                 sib_s, sib_r, y_s, y_r, rel_s, rel_r, gz_s, gz_r, gx_s, gx_r, ref_s, ref_r, ex_s, ex_r, loc,
                 c_s, c_r, x_s, x_r, z_s, z_r, y1_s, y1_r, y2_s, y2_r,
                 a1_s, a1_r, a2_s, a2_r, q_s, q_r, qq_s, qq_r, g_s, g_r, gg_s, gg_r, e_s, e_r):
    at = Place()
    y, zl, core, p, me = at.y, at.zl, at.core, at.parity, at.frame
    x, zh, oz = at.x, at.zh, 1 - at.zl
    for i, w in enumerate((w0, w1, w2, None, w4, w5, w6)):
        if w is not None:
            pack[i] = w[...]
    for i, w in ((3, w3), (7, w7)):
        wide = w[...].astype(F32)
        pack[i] = jnp.concatenate([wide[:, :640], wide[:, 640:]], 0).astype(BF)
    small = ref_in[...].astype(F32)
    ref8[...] = jnp.concatenate([small, small[:2] * 0.0], 0).astype(BF)
    greet([at.peer(i) for i in range(1, 16)] + [at.along_x(1), at.along_x(-1), at.along_z(1), at.along_z(-1),
                                                at.along_zh(1), at.along_zh(-1)])
    sends = []

    def go(copy):
        copy.start()
        sends.append(copy)
        return copy

    steps = (1, -1)
    fulls = (full_s, full_t)
    keeps = []

    def gather_chain(h):
        full = fulls[h]
        rows = [shard_of(y + k, zl, core) for k in range(4)]
        over = [shard_of(y + k, 1 - zl, core) for k in range(4)]

        def pair(j):
            return pl.ds(2 * j, 2)

        def to_sibling(index, ref):
            go(remote(ref, ref, sib_s.at[h, index], sib_r.at[h, index], at.sibling))

        def z_send(k, src=None):
            for d in range(2):
                w = 2 * p + d
                dst = full.at[rows[k], w]
                go(remote(dst if src is None else src.at[4 * h + w], dst, gz_s.at[h, k, d], gz_r.at[h, k, d],
                          at.along_z(1 - 2 * d)))

        def z_wait(k):
            for d in range(2):
                ref = full.at[over[k], 2 * p + d]
                remote(ref, ref, gz_s.at[h, k, d], gz_r.at[h, k, d], at.along_z(1)).wait_recv()
                go(remote(ref, ref, gx_s.at[h, k, d], gx_r.at[h, k, d], at.along_x(1 - 2 * d)))
                to_sibling(7 + 2 * k + d, ref)

        def x_wait(k):
            for d in range(2):
                ref = full.at[over[k], 2 * (1 - p) + d]
                remote(ref, ref, gx_s.at[h, k, d], gx_r.at[h, k, d], at.along_x(1)).wait_recv()
                to_sibling(15 + 2 * k + d, ref)

        half = pl.ds(4 * h, 4)
        for j in range(2):
            for s, step in enumerate(steps):
                go(remote(pack.at[pl.ds(4 * h + 2 * j, 2)], full.at[me, pair(j)], y_s.at[h, s, j], y_r.at[h, s, j],
                          at.along_y(step)))
        z_send(0, pack)
        go(remote(pack.at[half], full.at[me], sib_s.at[h, 0], sib_r.at[h, 0], at.sibling))
        keeps.append(load(pack.at[half], full.at[me], loc.at[h]))
        yield
        for j in range(2):
            for s, step in enumerate(steps):
                ref = full.at[rows[(4 - step) % 4], pair(j)]
                remote(ref, ref, y_s.at[h, s, j], y_r.at[h, s, j], at.along_y(step)).wait_recv()
                if j == s:
                    go(remote(ref, ref, rel_s.at[h, j], rel_r.at[h, j], at.along_y(step)))
                to_sibling(1 + 2 * s + j, ref)
        z_send(1)
        z_send(3)
        yield
        z_wait(0)
        for j in range(2):
            ref = full.at[rows[2], pair(j)]
            remote(ref, ref, rel_s.at[h, j], rel_r.at[h, j], at.along_y(1)).wait_recv()
            to_sibling(5 + j, ref)
        z_send(2)
        yield
        z_wait(1)
        z_wait(3)
        x_wait(0)
        yield
        z_wait(2)
        x_wait(1)
        x_wait(3)
        yield
        x_wait(2)
        yield

        def sib_wait(index, ref):
            remote(ref, ref, sib_s.at[h, index], sib_r.at[h, index], at.sibling).wait_recv()

        other = [shard_of(y + k, zl, 1 - core) for k in range(4)]
        sib_wait(0, full.at[other[0]])
        for s, step in enumerate(steps):
            for j in range(2):
                sib_wait(1 + 2 * s + j, full.at[other[(4 - step) % 4], pair(j)])
        for j in range(2):
            sib_wait(5 + j, full.at[other[2], pair(j)])
        for k in range(4):
            for d in range(2):
                far = shard_of(y + k, 1 - zl, 1 - core)
                sib_wait(7 + 2 * k + d, full.at[far, 2 * p + d])
                sib_wait(15 + 2 * k + d, full.at[far, 2 * (1 - p) + d])

    def rem4(v):
        return lax.rem(v + 8, 4)

    cross = {}

    def send_cross(h, w):
        src = dws if h == 0 else dwt
        for a, zz in enumerate((oz, zl)):
            cross[h, a, w] = go(remote(src.at[1 - core, zz, w], r0.at[h, a, w], c_s.at[h, a, w], c_r.at[h, a, w],
                                       at.sibling))

    def chain(h):
        g = (dws if h == 0 else dwt).at[core]
        low, high = pl.ds(0, 48), pl.ds(48, 32)
        ys = [rem4(y + k) for k in range(4)]
        xc, zc = {}, {}

        def take(a, zz):
            for w in range(4):
                cross[h, a, w].wait_recv()
                g[zz, w] = add(g[zz, w], r0[h, a, w]).astype(BF)

        def x_take(k):
            for d in range(2):
                xc[k, d].wait_recv()
                w = 2 * p + d
                g[oz, w, ys[k]] = add(g[oz, w, ys[k]], rx[h, d, k]).astype(BF)
                zc[k, d] = go(remote(g.at[oz, w, ys[k]], rz.at[h, d, k], z_s.at[h, d, k], z_r.at[h, d, k],
                                     at.along_z(2 * d - 1)))

        def z_take(k):
            for d in range(2):
                zc[k, d].wait_recv()
                w = 2 * p + d
                g[zl, w, ys[k]] = add(g[zl, w, ys[k]], rz[h, d, k]).astype(BF)

        take(0, oz)
        for k in (2, 1, 3, 0):
            for d in range(2):
                xc[k, d] = go(remote(g.at[oz, 2 * (1 - p) + d, ys[k]], rx.at[h, d, k], x_s.at[h, d, k],
                                     x_r.at[h, d, k], at.along_x(2 * d - 1)))
        take(1, zl)
        yield
        x_take(2)
        yield
        x_take(1)
        yield
        z_take(2)
        y1 = [go(remote(g.at[zl, w, ys[2]], ry1.at[h, w], y1_s.at[h, w], y1_r.at[h, w],
                        at.along_y(-1 if w < 2 else 1))) for w in range(4)]
        yield
        x_take(3)
        x_take(0)
        yield
        z_take(1)
        z_take(3)
        yield
        for w in range(4):
            y1[w].wait_recv()
            on = ys[3 if w < 2 else 1]
            g[zl, w, on] = add(g[zl, w, on], ry1[h, w]).astype(BF)
        y2 = {}
        turn = [rem4(x + 2), rem4(x + 1), rem4(x + 3), x]
        for n, w in enumerate(turn):
            for s, step in enumerate((1, -1)):
                y2[s, n] = go(remote(g.at[zl, w, ys[step % 4]], ry2.at[s, h, n], y2_s.at[s, h, n],
                                     y2_r.at[s, h, n], at.along_y(step)))
        yield
        z_take(0)
        yield

        def y_take(n):
            y2[0, n].wait_recv()
            y2[1, n].wait_recv()
            pm[h, n] = add(g[zl, turn[n], y], ry2[0, h, n], ry2[1, h, n]).astype(BF)

        y_take(0)
        a1 = [go(remote(pm.at[h, 0, part], rax1.at[h, part], a1_s.at[h, s], a1_r.at[h, s], at.along_x(step)))
              for s, (step, part) in enumerate(((1, low), (-1, high)))]
        yield
        y_take(1)
        y_take(2)
        a2 = []
        for s, (step, part) in enumerate(((1, low), (-1, high))):
            a1[s].wait_recv()
            pm[h, 1 + s, part] = add(pm[h, 1 + s, part], rax1[h, part]).astype(BF)
            a2.append(go(remote(pm.at[h, 1 + s], rax2.at[s, h], a2_s.at[h, s], a2_r.at[h, s], at.along_x(step))))
        yield
        y_take(3)
        for copy in a2:
            copy.wait_recv()
        rq[h, zh] = add(pm[h, 3], rax2[0, h], rax2[1, h]).astype(BF)
        for s, step in enumerate((1, -1)):
            go(remote(rq.at[h, zh], rq.at[h, zh], q_s.at[h, s], q_r.at[h, s], at.along_zh(step)))
        yield
        for s, (step, part) in enumerate(((1, low), (-1, high))):
            ref = rq.at[h, rem4(zh - step)]
            remote(ref, ref, q_s.at[h, s], q_r.at[h, s], at.along_zh(step)).wait_recv()
            ref = rq.at[h, rem4(zh - step), part]
            go(remote(ref, ref, qq_s.at[h, s], qq_r.at[h, s], at.along_zh(step)))
        yield
        for s, (step, part) in enumerate(((1, low), (-1, high))):
            ref = rq.at[h, rem4(zh + 2), part]
            remote(ref, ref, qq_s.at[h, s], qq_r.at[h, s], at.along_zh(step)).wait_recv()
        fin[h, x] = add(rq[h, 0], rq[h, 1], rq[h, 2], rq[h, 3]).astype(BF)
        for s, step in enumerate((1, -1)):
            go(remote(fin.at[h, x], fin.at[h, x], g_s.at[h, s], g_r.at[h, s], at.along_x(step)))
        yield
        for s, (step, part) in enumerate(((1, low), (-1, high))):
            ref = fin.at[h, rem4(x - step)]
            remote(ref, ref, g_s.at[h, s], g_r.at[h, s], at.along_x(step)).wait_recv()
            ref = fin.at[h, rem4(x - step), part]
            go(remote(ref, ref, gg_s.at[h, s], gg_r.at[h, s], at.along_x(step)))
        yield
        for s, (step, part) in enumerate(((1, low), (-1, high))):
            ref = fin.at[h, rem4(x + 2), part]
            remote(ref, ref, gg_s.at[h, s], gg_r.at[h, s], at.along_x(step)).wait_recv()
        yield

    now, later = gather_chain(0), gather_chain(1)
    next(now)
    pack_rows = frame_pack()
    buf_g[...] = dot(pack_rows, og_in[...]).astype(BF)
    masks = head_masks()
    wide = frames[...].astype(F32)
    n1 = stats(wide)[0].astype(BF)
    next(now)
    for i in range(1, 16):
        go(remote(ref8, refs.at[me], ref_s.at[i], ref_r.at[i], at.peer(i)))
    refs[me] = ref8[...]
    next(now)
    next(later)
    next(now)
    next(now)
    next(now)
    for i in range(1, 16):
        ref = refs.at[lax.rem(me + 16 - i, 16)]
        remote(ref, ref, ref_s.at[i], ref_r.at[i], at.peer(i)).wait_recv()
    for _ in now:
        pass
    keeps[0].wait()
    ref = dot(ref_unpack(96, 128), refs[...].astype(F32).reshape(128, 1280).astype(BF)).astype(BF)
    q = dot(n1, full_s[:, 0].reshape(1280, 640)).astype(BF)
    w = full_s[:, 1].reshape(1280, 640)
    k, rk = dot(n1, w).astype(BF), dot(ref, w).astype(BF)
    next(later)
    w = full_s[:, 2].reshape(1280, 640)
    v, rv = dot(n1, w).astype(BF), dot(ref, w).astype(BF)
    for i, part in enumerate((q, k, v)):
        qkv[i] = part
    rkv[0] = rk
    rkv[1] = rv
    outs = []
    for a in range(2):
        rows = slice(96 * a, 96 * a + 96)
        keys = jnp.concatenate([k[rows], rk], 0)
        values = jnp.concatenate([v[rows], rv], 0)
        probs = softmax(stack_heads(q[rows], masks), keys).astype(BF)
        outs.append(merge_heads(dot(probs, values), masks))
        next(later)
    o = jnp.concatenate(outs, 0).astype(BF)
    o_in[...] = o
    left, right = wide_output(full_s[:, 3])
    h1 = (wide + jnp.concatenate([dot(o, left), dot(o, right)], 1)).astype(BF)
    h1_in[...] = h1
    buf_b[...] = dot(pack_rows, h1).astype(BF)
    copies = exchange_start(at, buf_b, h1r, ex_s.at[0], ex_r.at[0])
    to_owner = exchange_start(at, buf_g, ogr, ex_s.at[1], ex_r.at[1])
    for _ in later:
        pass
    for keep in keeps[1:]:
        keep.wait()
    for copy in copies:
        copy.wait_recv()
    unpack, t_pack = token_unpack(), token_pack()
    h1 = dot(unpack, h1r[...])
    centred, inverse = stats(h1)
    n2 = (centred + jnp.concatenate([table[...]] * 6, 0)).astype(BF)
    parts = []
    for i in range(3):
        parts.append(dot(n2, full_t[:, i].reshape(1280, 640)).astype(BF))
    q, k, v = parts
    r, c = iota((768, 192), 0), iota((768, 192), 1)
    r = jnp.where(r >= 384, r - 384, r)
    r = jnp.where(r >= 192, r - 192, r)
    same = lax.shift_right_logical(r, 5) == lax.shift_right_logical(c, 5)
    qs = stack_heads(q, masks)
    probs = softmax(qs, k, same)
    pb = probs.astype(BF)
    o2 = merge_heads(dot(pb, v), masks).astype(BF)
    buf_o[...] = dot(t_pack, o2).astype(BF)
    to_frame = exchange_start(at, buf_o, o2r, ex_s.at[2], ex_r.at[2])
    left, right = wide_output(full_t[:, 3])
    for copy in to_owner:
        copy.wait_recv()
    og = dot(unpack, ogr[...]).astype(BF)
    go2 = (dot(og[:, :640], left, 1, 1) + dot(og[:, 640:], right, 1, 1)).astype(BF)
    gs = stack_heads(go2, masks)
    eb = score_back(probs, gs, v)
    gq = merge_heads(dot(eb, k), masks).astype(BF)
    gk = dot(eb, qs, 0, 0).astype(BF)
    gv = dot(pb, gs, 0, 0).astype(BF)
    grads = (gq, gk, gv)
    gn = dot(gq, full_t[:, 0].reshape(1280, 640), 1, 1)
    for i in (1, 2):
        gn = gn + dot(grads[i], full_t[:, i].reshape(1280, 640), 1, 1)
    gh = (og.astype(F32) + stats_back(centred, inverse, gn)).astype(BF)
    buf[...] = dot(t_pack, gh).astype(BF)
    to_frame += exchange_start(at, buf, backr, ex_s.at[3], ex_r.at[3])
    for i in range(3):
        store_term(dwt, i, dot(n2, grads[i], 0, 0))
        send_cross(1, i)
    store_term(dwt, 3, pack_output(dot(o2, og[:, :640], 0, 0), dot(o2, og[:, 640:], 0, 0)))
    send_cross(1, 3)
    early = chain(1)
    for copy in to_frame:
        copy.wait_recv()
    f_unpack = frame_unpack()
    gh = dot(f_unpack, backr[...]).astype(BF)
    next(early)
    left, right = wide_output(full_s[:, 3])
    go_ = (dot(gh[:, :640], left, 1, 1) + dot(gh[:, 640:], right, 1, 1)).astype(BF)
    rk, rv = rkv[0], rkv[1]
    gq, gk, gv = [], [], []
    grk = grv = None
    for a in range(2):
        rows = slice(96 * a, 96 * a + 96)
        keys = jnp.concatenate([qkv[1, rows], rk], 0)
        values = jnp.concatenate([qkv[2, rows], rv], 0)
        qs = stack_heads(qkv[0, rows], masks)
        gs = stack_heads(go_[rows], masks)
        probs = softmax(qs, keys)
        eb = score_back(probs, gs, values)
        gq.append(merge_heads(dot(eb, keys), masks))
        gkeys = dot(eb, qs, 0, 0)
        gvalues = dot(probs.astype(BF), gs, 0, 0)
        gk.append(gkeys[:96])
        gv.append(gvalues[:96])
        grk = gkeys[96:] if grk is None else grk + gkeys[96:]
        grv = gvalues[96:] if grv is None else grv + gvalues[96:]
        next(early)
        next(early)
    gq, gk, gv = (jnp.concatenate(g, 0).astype(BF) for g in (gq, gk, gv))
    grk, grv = grk.astype(BF), grv.astype(BF)
    centred, inverse = stats(frames[...].astype(F32))
    n1 = centred.astype(BF)
    o = o_in[...]
    store_term(dws, 3, pack_output(dot(o, gh[:, :640], 0, 0), dot(o, gh[:, 640:], 0, 0)))
    send_cross(0, 3)
    store_term(dws, 0, dot(n1, gq, 0, 0))
    send_cross(0, 0)
    store_term(dws, 1, dot(n1, gk, 0, 0) + dot(ref, grk, 0, 0))
    send_cross(0, 1)
    store_term(dws, 2, dot(n1, gv, 0, 0) + dot(ref, grv, 0, 0))
    send_cross(0, 2)
    spread = ref_unpack(128, 96, True)
    gr[:, :, :640] = dot(spread, grk).reshape(16, 8, 640).astype(BF)
    gr[:, :, 640:] = dot(spread, grv).reshape(16, 8, 640).astype(BF)
    rgr[me] = gr[me]
    late = chain(0)
    next(late)
    next(early)
    for i in range(1, 16):
        to = lax.rem(me + i, 16)
        go(remote(gr.at[to], rgr.at[me], e_s.at[i], e_r.at[i], at.peer(i)))

    def finish_rows():
        gn = None
        for n, (i, g) in enumerate(((0, gq), (1, gk), (2, gv))):
            term = dot(g, full_s[:, n].reshape(1280, 640), 1, 1)
            gn = term if gn is None else gn + term
        fg_o[...] = (gh.astype(F32) + stats_back(centred, inverse, gn)).astype(BF)

    def finish_out():
        left, right = wide_output(full_t[:, 3])
        o2 = dot(f_unpack, o2r[...]).astype(BF)
        out_o[...] = (h1_in[...].astype(F32) + jnp.concatenate([dot(o2, left), dot(o2, right)], 1)).astype(BF)

    def finish_ref():
        for i in range(1, 16):
            got = rgr.at[lax.rem(me + 16 - i, 16)]
            remote(got, got, e_s.at[i], e_r.at[i], at.peer(i)).wait_recv()
        total = rgr[0].astype(F32)
        for i in range(1, 16):
            total = total + rgr[i].astype(F32)
        total = total.astype(BF)
        rg[...] = (dot(total[:, :640], full_s[:, 1].reshape(1280, 640), 1, 1)
                   + dot(total[:, 640:], full_s[:, 2].reshape(1280, 640), 1, 1)).astype(BF)

    work = {"A": finish_rows, "B": finish_out, "C": finish_ref}
    for step in "TTATSTSSBTSSSCSTSSTSTSTSSS":
        if step in work:
            work[step]()
        else:
            next(early if step == "T" else late)
    for copy in copies + to_owner + to_frame + sends:
        copy.wait_send()


def whole(frames, ref_in, og, table, weights):
    dma = pltpu.SemaphoreType.DMA
    s = jax.ShapeDtypeStruct
    v = pltpu.VMEM
    b = (80, 640)
    wide = v((256, 1280), BF)
    return pl.pallas_call(
        whole_kernel,
        out_shape=(s((192, 1280), BF), s((192, 1280), BF), s((8, 1280), BF), s((2, 4) + b, BF)),
        in_specs=[VM] * 12,
        out_specs=(VM,) * 4,
        scratch_shapes=[v((8,) + b, BF), v((8, 1280), BF), v((16, 4) + b, BF), v((16, 4) + b, BF),
                        v((16, 8, 1280), BF), v((3, 192, 640), BF), v((2, 96, 640), BF), v((192, 640), BF),
                        v((192, 1280), BF), wide, wide, wide, wide, v((256, 640), BF), v((256, 640), BF), wide, wide,
                        v((2, 2, 4, 4) + b, BF), v((2, 2, 4, 4) + b, BF), v((2, 2, 4, 4) + b, BF),
                        v((2, 2, 4) + b, BF), v((2, 2, 4) + b, BF), v((2, 4) + b, BF), v((2, 2, 4) + b, BF),
                        v((2, 4) + b, BF), v((2,) + b, BF), v((2, 2) + b, BF), v((2, 4) + b, BF),
                        v((16, 8, 1280), BF), v((16, 8, 1280), BF)]
        + [dma((2, 23))] * 2 + [dma((2, 2, 2))] * 2 + [dma((2, 2))] * 2 + [dma((2, 4, 2))] * 4 + [dma((16,))] * 2
        + [dma((4, 16))] * 2 + [dma((2,))]
        + [dma((2, 2, 4))] * 6 + [dma((2, 4))] * 2 + [dma((2, 2, 4))] * 2 + [dma((2, 2))] * 12 + [dma((16,))] * 2,
        compiler_params=pltpu.CompilerParams(collective_id=0, has_side_effects=True,
                                             vmem_limit_bytes=67043328),
        name="whole",
    )(frames, ref_in, og, table, *weights)


def finish_kernel(out, fg, rg, fin, out_o, fg_o, rg_o, *totals):
    out_o[...] = out[...]
    fg_o[...] = fg[...]
    rg_o[...] = rg[...].astype(F32)[:6].astype(BF)
    for h in range(2):
        for w in range(3):
            totals[4 * h + w][...] = fin[h, w].astype(F32)
        wide = fin[h, 3].astype(F32)
        totals[4 * h + 3][:, :640] = wide[:40]
        totals[4 * h + 3][:, 640:] = wide[40:]


def finish(out, fg, rg, fin):
    s = jax.ShapeDtypeStruct
    tall, flat = s((80, 640), F32), s((40, 1280), F32)
    return pl.pallas_call(
        finish_kernel,
        out_shape=(s((192, 1280), BF), s((192, 1280), BF), s((6, 1280), BF)) + (tall, tall, tall, flat) * 2,
        in_specs=[VM] * 4, out_specs=(VM,) * 11, name="write_outputs",
    )(out, fg, rg, fin)

def position_table(count, width):
    column = lax.broadcasted_iota(jnp.int32, (count, width), 1)
    frame = lax.broadcasted_iota(jnp.int32, (count, width), 0).astype(F32)
    rates = jnp.exp((column // 2).astype(F32) * (-2.0 * math.log(10000.0) / width))
    angles = frame * rates
    return jnp.where(column % 2 == 0, jnp.sin(angles), jnp.cos(angles))


def per_device(frames_in, ref_feats, out_grad, *weights):
    frames, grads = frames_in.reshape(192, 1280), out_grad.reshape(192, 1280)
    results = whole(frames, ref_feats[0], grads, position_table(32, 1280), weights)
    out, frames_grad, rg, *totals = finish(*results)
    return (out.reshape(frames_in.shape), frames_grad.reshape(frames_in.shape), rg[None], *totals)


def solution(mesh):
    rows, refs, weight = P("clip", "frame", None, None), P("clip", "frame", None), P("frame", None)
    return jax.shard_map(
        per_device, mesh=mesh, in_specs=(rows, refs, rows) + (weight,) * 8,
        out_specs=(rows, rows, refs) + (weight,) * 8, check_vma=False)
```

```python
import math

import jax
import jax.numpy as jnp
from jax import lax
from jax.experimental import pallas as pl
from jax.experimental.pallas import tpu as pltpu
from jax.sharding import PartitionSpec as P


MESH = pl.DeviceIdType.MESH
ANY = pl.BlockSpec(memory_space=pl.ANY)
VM = pl.BlockSpec(memory_space=pltpu.VMEM)


class Place:
    def __init__(self):
        clip, frame = lax.axis_index("clip"), lax.axis_index("frame")
        self.clip, self.frame = clip, frame
        self.x, self.zh = lax.rem(clip, 4), lax.div(clip, 4)
        self.y, self.zl, self.core = lax.div(frame, 4), lax.rem(lax.div(frame, 2), 2), lax.rem(frame, 2)
        self.parity = lax.rem(self.x, 2)
        self.sibling = (clip, frame + 1 - 2 * self.core)

    def along_y(self, step):
        return (self.clip, lax.rem(self.y + 4 + step, 4) * 4 + self.zl * 2 + self.core)

    def along_x(self, step):
        return (self.zh * 4 + lax.rem(self.x + 4 + step, 4), self.frame)

    def along_z(self, step):
        far = lax.rem(self.zh * 2 + self.zl + 8 + step, 8)
        return (lax.div(far, 2) * 4 + self.x, self.y * 4 + lax.rem(far, 2) * 2 + self.core)

    def along_zh(self, step):
        return (lax.rem(self.zh + 4 + step, 4) * 4 + self.x, self.frame)

    def peer(self, step):
        return (self.clip, lax.rem(self.frame + step, 16))


def greet(devices):
    barrier = pltpu.get_barrier_semaphore()
    for device in devices:
        pl.semaphore_signal(barrier, inc=1, device_id=device, device_id_type=MESH)
    pl.semaphore_wait(barrier, len(devices))


def remote(src, dst, send, recv, device):
    return pltpu.make_async_remote_copy(
        src_ref=src, dst_ref=dst, send_sem=send, recv_sem=recv, device_id=device, device_id_type=MESH)


def shard_of(y, zl, core):
    return lax.rem(y + 8, 4) * 4 + zl * 2 + core


BF, F32 = jnp.bfloat16, jnp.float32
EPSILON = 1e-05
SCALE = 160 ** -0.5


def dot(a, b, ca=1, cb=0):
    return lax.dot_general(a, b, (((ca,), (cb,)), ((), ())), preferred_element_type=F32)


def stats(wide):
    offset = wide - jnp.mean(wide, -1, keepdims=True)
    inverse = lax.rsqrt(jnp.mean(offset * offset, -1, keepdims=True) + EPSILON)
    return offset * inverse, inverse


def stats_back(centred, inverse, g):
    first = jnp.mean(g, -1, keepdims=True)
    second = jnp.mean(g * centred, -1, keepdims=True)
    return inverse * (g - first - centred * second)


def iota(shape, dim):
    return lax.broadcasted_iota(jnp.int32, shape, dim)


def one_hot(hit):
    return jnp.where(hit, 1.0, 0.0).astype(BF)


def frame_pack():
    r, c = iota((256, 192), 0), iota((256, 192), 1)
    d, j = lax.shift_right_logical(r, 4), lax.bitwise_and(r, 15)
    a = jnp.where(j >= 6, 1, 0)
    return one_hot((j < 12) & (c == 90 * a + 6 * d + j))


def frame_unpack():
    c, r = iota((192, 256), 0), iota((192, 256), 1)
    d, j = lax.shift_right_logical(r, 4), lax.bitwise_and(r, 15)
    a = jnp.where(j >= 6, 1, 0)
    return one_hot((j < 12) & (c == 90 * a + 6 * d + j))


def token_unpack():
    m, r = iota((192, 256), 0), iota((192, 256), 1)
    t, f, a = lax.shift_right_logical(m, 5), lax.bitwise_and(lax.shift_right_logical(m, 1), 15), lax.bitwise_and(m, 1)
    return one_hot(r == 16 * f + 6 * a + t)


def token_pack():
    m, r = iota((256, 192), 1), iota((256, 192), 0)
    t, f, a = lax.shift_right_logical(m, 5), lax.bitwise_and(lax.shift_right_logical(m, 1), 15), lax.bitwise_and(m, 1)
    return one_hot(r == 16 * f + 6 * a + t)


def ref_unpack(rows, cols, swap=False):
    m, r = (iota((rows, cols), 0), iota((rows, cols), 1)) if not swap else (iota((rows, cols), 1), iota((rows, cols), 0))
    d, j = lax.shift_right_logical(r, 3), lax.bitwise_and(r, 7)
    return one_hot((j < 6) & (m == 6 * d + j))


def head_masks():
    lane = iota((1, 640), 1)
    return [(lane >= 160 * h) & (lane < 160 * (h + 1)) for h in range(4)]


def stack_heads(rows, masks):
    return jnp.concatenate([rows * one_hot(m) for m in masks], 0)


def merge_heads(stacked, masks):
    n = stacked.shape[0] // 4
    total = jnp.where(masks[0], stacked[:n], 0.0)
    for h in range(1, 4):
        total = jnp.where(masks[h], stacked[h * n:(h + 1) * n], total)
    return total


def softmax(stacked, keys, same=None):
    powers = jnp.exp(dot(stacked, keys, 1, 1) * SCALE)
    if same is not None:
        powers = jnp.where(same, powers, 0.0)
    return powers / jnp.sum(powers, -1, keepdims=True)


def score_back(probs, grads, values):
    dp = dot(grads, values, 1, 1)
    return (probs * (dp - jnp.sum(probs * dp, -1, keepdims=True)) * SCALE).astype(BF)


def wide_output(slot):
    wide = slot.astype(F32)
    left = wide[:, :40].reshape(640, 640).astype(BF)
    right = wide[:, 40:].reshape(640, 640).astype(BF)
    return left, right


def pack_output(left, right):
    return jnp.concatenate([left.reshape(16, 40, 640), right.reshape(16, 40, 640)], 1)


def store_term(dw, w, term):
    parts = term.reshape(4, 2, 2, 80, 640).astype(BF)
    for core in range(2):
        for zl in range(2):
            dw[core, zl, w] = parts[:, zl, core]


def exchange_start(at, src, dst, send, recv):
    copies = []
    for i in range(1, 16):
        to = lax.rem(at.frame + i, 16)
        copy = remote(src.at[pl.ds(pl.multiple_of(16 * to, 16), 16)],
                      dst.at[pl.ds(pl.multiple_of(16 * at.frame, 16), 16)], send.at[i], recv.at[i], at.peer(i))
        copy.start()
        copies.append(copy)
    own = pl.ds(pl.multiple_of(16 * at.frame, 16), 16)
    dst[own, :] = src[own, :]
    return copies


def load(src, dst, sem):
    copy = pltpu.make_async_copy(src, dst, sem)
    copy.start()
    return copy


def add(*parts):
    total = parts[0].astype(F32)
    for part in parts[1:]:
        total = total + part.astype(F32)
    return total


def position_table(count, width):
    column = lax.broadcasted_iota(jnp.int32, (count, width), 1)
    frame = lax.broadcasted_iota(jnp.int32, (count, width), 0).astype(F32)
    rates = jnp.exp((column // 2).astype(F32) * (-2.0 * math.log(10000.0) / width))
    angles = frame * rates
    return jnp.where(column % 2 == 0, jnp.sin(angles), jnp.cos(angles))


ORDER = "SSTTSSATSTSSBTSSCTSTSTTSSS"


def whole_kernel(frames, ref_in, og_in, w0, w1, w2, w3, w4, w5, w6, w7,
                 out_o, fg_o, rg, fin,
                 pack, ref8, full_s, full_t, refs, qkv, rkv, o_in, h1_in,
                 table, buf_b, h1r, buf_g, ogr, buf_o, o2r, buf, backr,
                 dws, dwt, r0, rx, rz, ry1, ry2, pm, rax1, rax2, rq, gr, rgr,
                 sib_s, sib_r, y_s, y_r, rel_s, rel_r, gz_s, gz_r, gx_s, gx_r, ref_s, ref_r, ex_s, ex_r, loc,
                 c_s, c_r, x_s, x_r, z_s, z_r, y1_s, y1_r, y2_s, y2_r,
                 a1_s, a1_r, a2_s, a2_r, q_s, q_r, qq_s, qq_r, g_s, g_r, gg_s, gg_r, e_s, e_r):
    at = Place()
    y, zl, core, p, me = at.y, at.zl, at.core, at.parity, at.frame
    x, zh, oz = at.x, at.zh, 1 - at.zl
    for i, w in enumerate((w0, w1, w2, None, w4, w5, w6)):
        if w is not None:
            pack[i] = w[...]
    for i, w in ((3, w3), (7, w7)):
        wide = w[...].astype(F32)
        pack[i] = jnp.concatenate([wide[:, :640], wide[:, 640:]], 0).astype(BF)
    small = ref_in[...].astype(F32)
    ref8[...] = jnp.concatenate([small, small[:2] * 0.0], 0).astype(BF)
    greet([at.peer(i) for i in range(1, 16)] + [at.along_x(1), at.along_x(-1), at.along_z(1), at.along_z(-1),
                                                at.along_zh(1), at.along_zh(-1)])
    sends = []

    def go(copy):
        copy.start()
        sends.append(copy)
        return copy

    steps = (1, -1)
    fulls = (full_s, full_t)
    keeps = []

    def gather_chain(h):
        full = fulls[h]
        rows = [shard_of(y + k, zl, core) for k in range(4)]
        over = [shard_of(y + k, 1 - zl, core) for k in range(4)]

        def pair(j):
            return pl.ds(2 * j, 2)

        def to_sibling(index, ref):
            go(remote(ref, ref, sib_s.at[h, index], sib_r.at[h, index], at.sibling))

        def z_send(k, src=None):
            for d in range(2):
                w = 2 * p + d
                dst = full.at[rows[k], w]
                go(remote(dst if src is None else src.at[4 * h + w], dst, gz_s.at[h, k, d], gz_r.at[h, k, d],
                          at.along_z(1 - 2 * d)))

        def z_wait(k):
            for d in range(2):
                ref = full.at[over[k], 2 * p + d]
                remote(ref, ref, gz_s.at[h, k, d], gz_r.at[h, k, d], at.along_z(1)).wait_recv()
                go(remote(ref, ref, gx_s.at[h, k, d], gx_r.at[h, k, d], at.along_x(1 - 2 * d)))
                to_sibling(7 + 2 * k + d, ref)

        def x_wait(k):
            for d in range(2):
                ref = full.at[over[k], 2 * (1 - p) + d]
                remote(ref, ref, gx_s.at[h, k, d], gx_r.at[h, k, d], at.along_x(1)).wait_recv()
                to_sibling(15 + 2 * k + d, ref)

        half = pl.ds(4 * h, 4)
        for j in range(2):
            for s, step in enumerate(steps):
                go(remote(pack.at[pl.ds(4 * h + 2 * j, 2)], full.at[me, pair(j)], y_s.at[h, s, j], y_r.at[h, s, j],
                          at.along_y(step)))
        z_send(0, pack)
        go(remote(pack.at[half], full.at[me], sib_s.at[h, 0], sib_r.at[h, 0], at.sibling))
        keeps.append(load(pack.at[half], full.at[me], loc.at[h]))
        yield
        for j in range(2):
            for s, step in enumerate(steps):
                ref = full.at[rows[(4 - step) % 4], pair(j)]
                remote(ref, ref, y_s.at[h, s, j], y_r.at[h, s, j], at.along_y(step)).wait_recv()
                if j == s:
                    go(remote(ref, ref, rel_s.at[h, j], rel_r.at[h, j], at.along_y(step)))
                to_sibling(1 + 2 * s + j, ref)
        z_send(1)
        z_send(3)
        yield
        z_wait(0)
        for j in range(2):
            ref = full.at[rows[2], pair(j)]
            remote(ref, ref, rel_s.at[h, j], rel_r.at[h, j], at.along_y(1)).wait_recv()
            to_sibling(5 + j, ref)
        z_send(2)
        yield
        z_wait(1)
        z_wait(3)
        x_wait(0)
        yield
        z_wait(2)
        x_wait(1)
        x_wait(3)
        yield
        x_wait(2)
        yield

        def sib_wait(index, ref):
            remote(ref, ref, sib_s.at[h, index], sib_r.at[h, index], at.sibling).wait_recv()

        other = [shard_of(y + k, zl, 1 - core) for k in range(4)]
        sib_wait(0, full.at[other[0]])
        for s, step in enumerate(steps):
            for j in range(2):
                sib_wait(1 + 2 * s + j, full.at[other[(4 - step) % 4], pair(j)])
        for j in range(2):
            sib_wait(5 + j, full.at[other[2], pair(j)])
        for k in range(4):
            for d in range(2):
                far = shard_of(y + k, 1 - zl, 1 - core)
                sib_wait(7 + 2 * k + d, full.at[far, 2 * p + d])
                sib_wait(15 + 2 * k + d, full.at[far, 2 * (1 - p) + d])

    def rem4(v):
        return lax.rem(v + 8, 4)

    cross = {}

    def send_cross(h, w):
        src = dws if h == 0 else dwt
        for a, zz in enumerate((oz, zl)):
            cross[h, a, w] = go(remote(src.at[1 - core, zz, w], r0.at[h, a, w], c_s.at[h, a, w], c_r.at[h, a, w],
                                       at.sibling))

    def chain(h):
        g = (dws if h == 0 else dwt).at[core]
        low, high = pl.ds(0, 48), pl.ds(48, 32)
        ys = [rem4(y + k) for k in range(4)]
        xc, zc = {}, {}

        def take(a, zz, weights):
            for w in weights:
                cross[h, a, w].wait_recv()
                g[zz, w] = add(g[zz, w], r0[h, a, w]).astype(BF)

        def x_take(k):
            for d in range(2):
                xc[k, d].wait_recv()
                w = 2 * p + d
                g[oz, w, ys[k]] = add(g[oz, w, ys[k]], rx[h, d, k]).astype(BF)
                zc[k, d] = go(remote(g.at[oz, w, ys[k]], rz.at[h, d, k], z_s.at[h, d, k], z_r.at[h, d, k],
                                     at.along_z(2 * d - 1)))

        def z_take(k):
            for d in range(2):
                zc[k, d].wait_recv()
                w = 2 * p + d
                g[zl, w, ys[k]] = add(g[zl, w, ys[k]], rz[h, d, k]).astype(BF)

        take(0, oz, (0, 3))
        yield
        take(0, oz, (1, 2))
        for k in (2, 1, 3, 0):
            for d in range(2):
                xc[k, d] = go(remote(g.at[oz, 2 * (1 - p) + d, ys[k]], rx.at[h, d, k], x_s.at[h, d, k],
                                     x_r.at[h, d, k], at.along_x(2 * d - 1)))
        take(1, zl, (0, 3, 1, 2))
        yield
        x_take(2)
        yield
        x_take(1)
        yield
        z_take(2)
        y1 = [go(remote(g.at[zl, w, ys[2]], ry1.at[h, w], y1_s.at[h, w], y1_r.at[h, w],
                        at.along_y(-1 if w < 2 else 1))) for w in range(4)]
        yield
        x_take(3)
        x_take(0)
        yield
        z_take(1)
        z_take(3)
        yield
        for w in range(4):
            y1[w].wait_recv()
            on = ys[3 if w < 2 else 1]
            g[zl, w, on] = add(g[zl, w, on], ry1[h, w]).astype(BF)
        y2 = {}
        turn = [rem4(x + 2), rem4(x + 1), rem4(x + 3), x]
        for n, w in enumerate(turn):
            for s, step in enumerate((1, -1)):
                y2[s, n] = go(remote(g.at[zl, w, ys[step % 4]], ry2.at[s, h, n], y2_s.at[s, h, n],
                                     y2_r.at[s, h, n], at.along_y(step)))
        yield
        z_take(0)
        yield

        def y_take(n):
            y2[0, n].wait_recv()
            y2[1, n].wait_recv()
            pm[h, n] = add(g[zl, turn[n], y], ry2[0, h, n], ry2[1, h, n]).astype(BF)

        y_take(0)
        a1 = [go(remote(pm.at[h, 0, part], rax1.at[h, part], a1_s.at[h, s], a1_r.at[h, s], at.along_x(step)))
              for s, (step, part) in enumerate(((1, low), (-1, high)))]
        yield
        y_take(1)
        y_take(2)
        a2 = []
        for s, (step, part) in enumerate(((1, low), (-1, high))):
            a1[s].wait_recv()
            pm[h, 1 + s, part] = add(pm[h, 1 + s, part], rax1[h, part]).astype(BF)
            a2.append(go(remote(pm.at[h, 1 + s], rax2.at[s, h], a2_s.at[h, s], a2_r.at[h, s], at.along_x(step))))
        yield
        y_take(3)
        for copy in a2:
            copy.wait_recv()
        rq[h, zh] = add(pm[h, 3], rax2[0, h], rax2[1, h]).astype(BF)
        both = ((1, low, high), (-1, high, low))
        for n in range(2):
            for s, (step, *parts) in enumerate(both):
                ref = rq.at[h, zh, parts[n]]
                go(remote(ref, ref, q_s.at[h, s, n], q_r.at[h, s, n], at.along_zh(step)))
        yield
        for s, (step, part, _) in enumerate(both):
            ref = rq.at[h, rem4(zh - step), part]
            remote(ref, ref, q_s.at[h, s, 0], q_r.at[h, s, 0], at.along_zh(step)).wait_recv()
            go(remote(ref, ref, qq_s.at[h, s], qq_r.at[h, s], at.along_zh(step)))
        yield
        for s, (step, part, rest) in enumerate(both):
            ref = rq.at[h, rem4(zh - step), rest]
            remote(ref, ref, q_s.at[h, s, 1], q_r.at[h, s, 1], at.along_zh(step)).wait_recv()
            ref = rq.at[h, rem4(zh + 2), part]
            remote(ref, ref, qq_s.at[h, s], qq_r.at[h, s], at.along_zh(step)).wait_recv()
        fin[h, x] = add(rq[h, 0], rq[h, 1], rq[h, 2], rq[h, 3]).astype(BF)
        for n in range(2):
            for s, (step, *parts) in enumerate(both):
                ref = fin.at[h, x, parts[n]]
                go(remote(ref, ref, g_s.at[h, s, n], g_r.at[h, s, n], at.along_x(step)))
        yield
        for s, (step, part, _) in enumerate(both):
            ref = fin.at[h, rem4(x - step), part]
            remote(ref, ref, g_s.at[h, s, 0], g_r.at[h, s, 0], at.along_x(step)).wait_recv()
            go(remote(ref, ref, gg_s.at[h, s], gg_r.at[h, s], at.along_x(step)))
        yield
        for s, (step, part, rest) in enumerate(both):
            ref = fin.at[h, rem4(x - step), rest]
            remote(ref, ref, g_s.at[h, s, 1], g_r.at[h, s, 1], at.along_x(step)).wait_recv()
            ref = fin.at[h, rem4(x + 2), part]
            remote(ref, ref, gg_s.at[h, s], gg_r.at[h, s], at.along_x(step)).wait_recv()
        yield

    now, later = gather_chain(0), gather_chain(1)
    next(now)
    pack_rows = frame_pack()
    buf_g[...] = dot(pack_rows, og_in[...]).astype(BF)
    masks = head_masks()
    wide = frames[...].astype(F32)
    n1 = stats(wide)[0].astype(BF)
    table[...] = position_table(32, 1280)
    next(now)
    for i in range(1, 16):
        go(remote(ref8, refs.at[me], ref_s.at[i], ref_r.at[i], at.peer(i)))
    refs[me] = ref8[...]
    next(now)
    next(later)
    next(now)
    next(now)
    next(now)
    for i in range(1, 16):
        ref = refs.at[lax.rem(me + 16 - i, 16)]
        remote(ref, ref, ref_s.at[i], ref_r.at[i], at.peer(i)).wait_recv()
    for _ in now:
        pass
    keeps[0].wait()
    ref = dot(ref_unpack(96, 128), refs[...].astype(F32).reshape(128, 1280).astype(BF)).astype(BF)
    q = dot(n1, full_s[:, 0].reshape(1280, 640)).astype(BF)
    w = full_s[:, 1].reshape(1280, 640)
    k, rk = dot(n1, w).astype(BF), dot(ref, w).astype(BF)
    next(later)
    w = full_s[:, 2].reshape(1280, 640)
    v, rv = dot(n1, w).astype(BF), dot(ref, w).astype(BF)
    for i, part in enumerate((q, k, v)):
        qkv[i] = part
    rkv[0] = rk
    rkv[1] = rv
    outs = []
    for a in range(2):
        rows = slice(96 * a, 96 * a + 96)
        keys = jnp.concatenate([k[rows], rk], 0)
        values = jnp.concatenate([v[rows], rv], 0)
        probs = softmax(stack_heads(q[rows], masks), keys).astype(BF)
        outs.append(merge_heads(dot(probs, values), masks))
        next(later)
    o = jnp.concatenate(outs, 0).astype(BF)
    o_in[...] = o
    left, right = wide_output(full_s[:, 3])
    h1 = (wide + jnp.concatenate([dot(o, left), dot(o, right)], 1)).astype(BF)
    h1_in[...] = h1
    buf_b[...] = dot(pack_rows, h1).astype(BF)
    copies = exchange_start(at, buf_b, h1r, ex_s.at[0], ex_r.at[0])
    to_owner = exchange_start(at, buf_g, ogr, ex_s.at[1], ex_r.at[1])
    for _ in later:
        pass
    for keep in keeps[1:]:
        keep.wait()
    for copy in copies:
        copy.wait_recv()
    unpack, t_pack = token_unpack(), token_pack()
    h1 = dot(unpack, h1r[...])
    centred, inverse = stats(h1)
    n2 = (centred + jnp.concatenate([table[...]] * 6, 0)).astype(BF)
    parts = []
    for i in range(3):
        parts.append(dot(n2, full_t[:, i].reshape(1280, 640)).astype(BF))
    q, k, v = parts
    r, c = iota((768, 192), 0), iota((768, 192), 1)
    r = jnp.where(r >= 384, r - 384, r)
    r = jnp.where(r >= 192, r - 192, r)
    same = lax.shift_right_logical(r, 5) == lax.shift_right_logical(c, 5)
    qs = stack_heads(q, masks)
    probs = softmax(qs, k, same)
    pb = probs.astype(BF)
    o2 = merge_heads(dot(pb, v), masks).astype(BF)
    buf_o[...] = dot(t_pack, o2).astype(BF)
    to_frame = exchange_start(at, buf_o, o2r, ex_s.at[2], ex_r.at[2])
    left, right = wide_output(full_t[:, 3])
    for copy in to_owner:
        copy.wait_recv()
    og = dot(unpack, ogr[...]).astype(BF)
    go2 = (dot(og[:, :640], left, 1, 1) + dot(og[:, 640:], right, 1, 1)).astype(BF)
    gs = stack_heads(go2, masks)
    eb = score_back(probs, gs, v)
    gq = merge_heads(dot(eb, k), masks).astype(BF)
    gk = dot(eb, qs, 0, 0).astype(BF)
    gv = dot(pb, gs, 0, 0).astype(BF)
    grads = (gq, gk, gv)
    gn = dot(gq, full_t[:, 0].reshape(1280, 640), 1, 1)
    for i in (1, 2):
        gn = gn + dot(grads[i], full_t[:, i].reshape(1280, 640), 1, 1)
    gh = (og.astype(F32) + stats_back(centred, inverse, gn)).astype(BF)
    buf[...] = dot(t_pack, gh).astype(BF)
    to_frame += exchange_start(at, buf, backr, ex_s.at[3], ex_r.at[3])
    for i in range(3):
        store_term(dwt, i, dot(n2, grads[i], 0, 0))
        send_cross(1, i)
    store_term(dwt, 3, pack_output(dot(o2, og[:, :640], 0, 0), dot(o2, og[:, 640:], 0, 0)))
    send_cross(1, 3)
    early = chain(1)
    next(early)
    for copy in to_frame:
        copy.wait_recv()
    f_unpack = frame_unpack()
    gh = dot(f_unpack, backr[...]).astype(BF)
    next(early)
    left, right = wide_output(full_s[:, 3])
    go_ = (dot(gh[:, :640], left, 1, 1) + dot(gh[:, 640:], right, 1, 1)).astype(BF)
    rk, rv = rkv[0], rkv[1]
    gq, gk, gv = [], [], []
    grk = grv = None
    for a in range(2):
        rows = slice(96 * a, 96 * a + 96)
        keys = jnp.concatenate([qkv[1, rows], rk], 0)
        values = jnp.concatenate([qkv[2, rows], rv], 0)
        qs = stack_heads(qkv[0, rows], masks)
        gs = stack_heads(go_[rows], masks)
        probs = softmax(qs, keys)
        eb = score_back(probs, gs, values)
        gq.append(merge_heads(dot(eb, keys), masks))
        gkeys = dot(eb, qs, 0, 0)
        gvalues = dot(probs.astype(BF), gs, 0, 0)
        gk.append(gkeys[:96])
        gv.append(gvalues[:96])
        grk = gkeys[96:] if grk is None else grk + gkeys[96:]
        grv = gvalues[96:] if grv is None else grv + gvalues[96:]
        next(early)
        next(early)
    gq, gk, gv = (jnp.concatenate(g, 0).astype(BF) for g in (gq, gk, gv))
    grk, grv = grk.astype(BF), grv.astype(BF)
    centred, inverse = stats(frames[...].astype(F32))
    n1 = centred.astype(BF)
    o = o_in[...]
    store_term(dws, 3, pack_output(dot(o, gh[:, :640], 0, 0), dot(o, gh[:, 640:], 0, 0)))
    send_cross(0, 3)
    store_term(dws, 0, dot(n1, gq, 0, 0))
    send_cross(0, 0)
    store_term(dws, 1, dot(n1, gk, 0, 0) + dot(ref, grk, 0, 0))
    send_cross(0, 1)
    late = chain(0)
    store_term(dws, 2, dot(n1, gv, 0, 0) + dot(ref, grv, 0, 0))
    send_cross(0, 2)
    next(late)
    next(late)
    spread = ref_unpack(128, 96, True)
    gr[:, :, :640] = dot(spread, grk).reshape(16, 8, 640).astype(BF)
    gr[:, :, 640:] = dot(spread, grv).reshape(16, 8, 640).astype(BF)
    rgr[me] = gr[me]
    next(early)
    for i in range(1, 16):
        to = lax.rem(me + i, 16)
        go(remote(gr.at[to], rgr.at[me], e_s.at[i], e_r.at[i], at.peer(i)))

    def finish_rows():
        gn = None
        for n, (i, g) in enumerate(((0, gq), (1, gk), (2, gv))):
            term = dot(g, full_s[:, n].reshape(1280, 640), 1, 1)
            gn = term if gn is None else gn + term
        fg_o[...] = (gh.astype(F32) + stats_back(centred, inverse, gn)).astype(BF)

    def finish_out():
        left, right = wide_output(full_t[:, 3])
        o2 = dot(f_unpack, o2r[...]).astype(BF)
        out_o[...] = (h1_in[...].astype(F32) + jnp.concatenate([dot(o2, left), dot(o2, right)], 1)).astype(BF)

    def finish_ref():
        for i in range(1, 16):
            got = rgr.at[lax.rem(me + 16 - i, 16)]
            remote(got, got, e_s.at[i], e_r.at[i], at.peer(i)).wait_recv()
        total = rgr[0].astype(F32)
        for i in range(1, 16):
            total = total + rgr[i].astype(F32)
        total = total.astype(BF)
        rg[...] = (dot(total[:, :640], full_s[:, 1].reshape(1280, 640), 1, 1)
                   + dot(total[:, 640:], full_s[:, 2].reshape(1280, 640), 1, 1)).astype(BF)

    work = {"A": finish_rows, "B": finish_out, "C": finish_ref}
    for step in ORDER:
        if step in work:
            work[step]()
        else:
            next(early if step == "T" else late)
    for copy in copies + to_owner + to_frame + sends:
        copy.wait_send()


def whole(frames, ref_in, og, weights):
    dma = pltpu.SemaphoreType.DMA
    s = jax.ShapeDtypeStruct
    v = pltpu.VMEM
    b = (80, 640)
    wide = v((256, 1280), BF)
    return pl.pallas_call(
        whole_kernel,
        out_shape=(s((192, 1280), BF), s((192, 1280), BF), s((8, 1280), BF), s((2, 4) + b, BF)),
        in_specs=[VM] * 11,
        out_specs=(VM,) * 4,
        scratch_shapes=[v((8,) + b, BF), v((8, 1280), BF), v((16, 4) + b, BF), v((16, 4) + b, BF),
                        v((16, 8, 1280), BF), v((3, 192, 640), BF), v((2, 96, 640), BF), v((192, 640), BF),
                        v((192, 1280), BF), v((32, 1280), F32), wide, wide, wide, wide, v((256, 640), BF), v((256, 640), BF), wide, wide,
                        v((2, 2, 4, 4) + b, BF), v((2, 2, 4, 4) + b, BF), v((2, 2, 4, 4) + b, BF),
                        v((2, 2, 4) + b, BF), v((2, 2, 4) + b, BF), v((2, 4) + b, BF), v((2, 2, 4) + b, BF),
                        v((2, 4) + b, BF), v((2,) + b, BF), v((2, 2) + b, BF), v((2, 4) + b, BF),
                        v((16, 8, 1280), BF), v((16, 8, 1280), BF)]
        + [dma((2, 23))] * 2 + [dma((2, 2, 2))] * 2 + [dma((2, 2))] * 2 + [dma((2, 4, 2))] * 4 + [dma((16,))] * 2
        + [dma((4, 16))] * 2 + [dma((2,))]
        + [dma((2, 2, 4))] * 6 + [dma((2, 4))] * 2 + [dma((2, 2, 4))] * 2 + [dma((2, 2))] * 4 + [dma((2, 2, 2))] * 2
        + [dma((2, 2))] * 2 + [dma((2, 2, 2))] * 2 + [dma((2, 2))] * 2 + [dma((16,))] * 2,
        compiler_params=pltpu.CompilerParams(collective_id=0, has_side_effects=True,
                                             vmem_limit_bytes=67043328),
        name="whole",
    )(frames, ref_in, og, *weights)


def finish_kernel(out, fg, rg, fin, out_o, fg_o, rg_o, *totals):
    out_o[...] = out[...]
    fg_o[...] = fg[...]
    rg_o[...] = rg[...].astype(F32)[:6].astype(BF)
    for h in range(2):
        for w in range(3):
            totals[4 * h + w][...] = fin[h, w].astype(F32)
        wide = fin[h, 3].astype(F32)
        totals[4 * h + 3][:, :640] = wide[:40]
        totals[4 * h + 3][:, 640:] = wide[40:]


def finish(out, fg, rg, fin):
    s = jax.ShapeDtypeStruct
    tall, flat = s((80, 640), F32), s((40, 1280), F32)
    return pl.pallas_call(
        finish_kernel,
        out_shape=(s((192, 1280), BF), s((192, 1280), BF), s((6, 1280), BF)) + (tall, tall, tall, flat) * 2,
        in_specs=[VM] * 4, out_specs=(VM,) * 11, name="write_outputs",
    )(out, fg, rg, fin)

def per_device(frames_in, ref_feats, out_grad, *weights):
    frames, grads = frames_in.reshape(192, 1280), out_grad.reshape(192, 1280)
    results = whole(frames, ref_feats[0], grads, weights)
    out, frames_grad, rg, *totals = finish(*results)
    return (out.reshape(frames_in.shape), frames_grad.reshape(frames_in.shape), rg[None], *totals)


def solution(mesh):
    rows, refs, weight = P("clip", "frame", None, None), P("clip", "frame", None), P("frame", None)
    return jax.shard_map(
        per_device, mesh=mesh, in_specs=(rows, refs, rows) + (weight,) * 8,
        out_specs=(rows, rows, refs) + (weight,) * 8, check_vma=False)
```

```python
import math

import jax
import jax.numpy as jnp
from jax import lax
from jax.experimental import pallas as pl
from jax.experimental.pallas import tpu as pltpu
from jax.sharding import PartitionSpec as P


MESH = pl.DeviceIdType.MESH
ANY = pl.BlockSpec(memory_space=pl.ANY)
VM = pl.BlockSpec(memory_space=pltpu.VMEM)


class Place:
    def __init__(self):
        clip, frame = lax.axis_index("clip"), lax.axis_index("frame")
        self.clip, self.frame = clip, frame
        self.x, self.zh = lax.rem(clip, 4), lax.div(clip, 4)
        self.y, self.zl, self.core = lax.div(frame, 4), lax.rem(lax.div(frame, 2), 2), lax.rem(frame, 2)
        self.parity = lax.rem(self.x, 2)
        self.sibling = (clip, frame + 1 - 2 * self.core)

    def along_y(self, step):
        return (self.clip, lax.rem(self.y + 4 + step, 4) * 4 + self.zl * 2 + self.core)

    def along_x(self, step):
        return (self.zh * 4 + lax.rem(self.x + 4 + step, 4), self.frame)

    def along_z(self, step):
        far = lax.rem(self.zh * 2 + self.zl + 8 + step, 8)
        return (lax.div(far, 2) * 4 + self.x, self.y * 4 + lax.rem(far, 2) * 2 + self.core)

    def along_zh(self, step):
        return (lax.rem(self.zh + 4 + step, 4) * 4 + self.x, self.frame)

    def peer(self, step):
        return (self.clip, lax.rem(self.frame + step, 16))


def greet(devices):
    barrier = pltpu.get_barrier_semaphore()
    for device in devices:
        pl.semaphore_signal(barrier, inc=1, device_id=device, device_id_type=MESH)
    pl.semaphore_wait(barrier, len(devices))


def remote(src, dst, send, recv, device):
    return pltpu.make_async_remote_copy(
        src_ref=src, dst_ref=dst, send_sem=send, recv_sem=recv, device_id=device, device_id_type=MESH)


def shard_of(y, zl, core):
    return lax.rem(y + 8, 4) * 4 + zl * 2 + core


BF, F32 = jnp.bfloat16, jnp.float32
EPSILON = 1e-05
SCALE = 160 ** -0.5


def dot(a, b, ca=1, cb=0):
    return lax.dot_general(a, b, (((ca,), (cb,)), ((), ())), preferred_element_type=F32)


def stats(wide):
    offset = wide - jnp.mean(wide, -1, keepdims=True)
    inverse = lax.rsqrt(jnp.mean(offset * offset, -1, keepdims=True) + EPSILON)
    return offset * inverse, inverse


def stats_back(centred, inverse, g):
    first = jnp.mean(g, -1, keepdims=True)
    second = jnp.mean(g * centred, -1, keepdims=True)
    return inverse * (g - first - centred * second)


def iota(shape, dim):
    return lax.broadcasted_iota(jnp.int32, shape, dim)


def one_hot(hit):
    return jnp.where(hit, 1.0, 0.0).astype(BF)


def frame_pack():
    r, c = iota((256, 192), 0), iota((256, 192), 1)
    d, j = lax.shift_right_logical(r, 4), lax.bitwise_and(r, 15)
    a = jnp.where(j >= 6, 1, 0)
    return one_hot((j < 12) & (c == 90 * a + 6 * d + j))


def frame_unpack():
    c, r = iota((192, 256), 0), iota((192, 256), 1)
    d, j = lax.shift_right_logical(r, 4), lax.bitwise_and(r, 15)
    a = jnp.where(j >= 6, 1, 0)
    return one_hot((j < 12) & (c == 90 * a + 6 * d + j))


def token_unpack():
    m, r = iota((192, 256), 0), iota((192, 256), 1)
    t, f, a = lax.shift_right_logical(m, 5), lax.bitwise_and(lax.shift_right_logical(m, 1), 15), lax.bitwise_and(m, 1)
    return one_hot(r == 16 * f + 6 * a + t)


def token_pack():
    m, r = iota((256, 192), 1), iota((256, 192), 0)
    t, f, a = lax.shift_right_logical(m, 5), lax.bitwise_and(lax.shift_right_logical(m, 1), 15), lax.bitwise_and(m, 1)
    return one_hot(r == 16 * f + 6 * a + t)


def ref_unpack(rows, cols, swap=False):
    m, r = (iota((rows, cols), 0), iota((rows, cols), 1)) if not swap else (iota((rows, cols), 1), iota((rows, cols), 0))
    d, j = lax.shift_right_logical(r, 3), lax.bitwise_and(r, 7)
    return one_hot((j < 6) & (m == 6 * d + j))


def head_masks():
    lane = iota((1, 640), 1)
    return [(lane >= 160 * h) & (lane < 160 * (h + 1)) for h in range(4)]


def stack_heads(rows, masks):
    return jnp.concatenate([rows * one_hot(m) for m in masks], 0)


def merge_heads(stacked, masks):
    n = stacked.shape[0] // 4
    total = jnp.where(masks[0], stacked[:n], 0.0)
    for h in range(1, 4):
        total = jnp.where(masks[h], stacked[h * n:(h + 1) * n], total)
    return total


def softmax(stacked, keys, same=None):
    powers = jnp.exp(dot(stacked, keys, 1, 1) * SCALE)
    if same is not None:
        powers = jnp.where(same, powers, 0.0)
    return powers / jnp.sum(powers, -1, keepdims=True)


def score_back(probs, grads, values):
    dp = dot(grads, values, 1, 1)
    return (probs * (dp - jnp.sum(probs * dp, -1, keepdims=True)) * SCALE).astype(BF)


def wide_output(slot):
    wide = slot.astype(F32)
    left = wide[:, :40].reshape(640, 640).astype(BF)
    right = wide[:, 40:].reshape(640, 640).astype(BF)
    return left, right


def pack_output(left, right):
    return jnp.concatenate([left.reshape(16, 40, 640), right.reshape(16, 40, 640)], 1)


def store_term(dw, w, term):
    parts = term.reshape(4, 2, 2, 80, 640).astype(BF)
    for core in range(2):
        for zl in range(2):
            dw[core, zl, w] = parts[:, zl, core]


def exchange_start(at, src, dst, send, recv):
    copies = []
    for i in range(1, 16):
        to = lax.rem(at.frame + i, 16)
        copy = remote(src.at[pl.ds(pl.multiple_of(16 * to, 16), 16)],
                      dst.at[pl.ds(pl.multiple_of(16 * at.frame, 16), 16)], send.at[i], recv.at[i], at.peer(i))
        copy.start()
        copies.append(copy)
    own = pl.ds(pl.multiple_of(16 * at.frame, 16), 16)
    dst[own, :] = src[own, :]
    return copies


def load(src, dst, sem):
    copy = pltpu.make_async_copy(src, dst, sem)
    copy.start()
    return copy


def add(*parts):
    total = parts[0].astype(F32)
    for part in parts[1:]:
        total = total + part.astype(F32)
    return total


def position_table(count, width):
    column = lax.broadcasted_iota(jnp.int32, (count, width), 1)
    frame = lax.broadcasted_iota(jnp.int32, (count, width), 0).astype(F32)
    rates = jnp.exp((column // 2).astype(F32) * (-2.0 * math.log(10000.0) / width))
    angles = frame * rates
    return jnp.where(column % 2 == 0, jnp.sin(angles), jnp.cos(angles))


ORDER = "ASSTTSBSTSTSSTSSCTSTSTTSSS"


def whole_kernel(frames, ref_in, og_in, w0, w1, w2, w3, w4, w5, w6, w7,
                 out_o, fg_o, rg, fin,
                 pack, ref8, full_s, full_t, refs, qkv, rkv, o_in, h1_in,
                 table, buf_b, h1r, buf_g, ogr, buf_o, o2r, buf, backr,
                 dws, dwt, r0, rx, rz, ry1, ry2, pm, rax1, rax2, rq, gr, rgr,
                 sib_s, sib_r, y_s, y_r, rel_s, rel_r, gz_s, gz_r, gx_s, gx_r, ref_s, ref_r, ex_s, ex_r, loc,
                 c_s, c_r, x_s, x_r, z_s, z_r, y1_s, y1_r, y2_s, y2_r,
                 a1_s, a1_r, a2_s, a2_r, q_s, q_r, qq_s, qq_r, g_s, g_r, gg_s, gg_r, e_s, e_r):
    at = Place()
    y, zl, core, p, me = at.y, at.zl, at.core, at.parity, at.frame
    x, zh, oz = at.x, at.zh, 1 - at.zl
    for i, w in enumerate((w0, w1, w2, None, w4, w5, w6)):
        if w is not None:
            pack[i] = w[...]
    for i, w in ((3, w3), (7, w7)):
        wide = w[...].astype(F32)
        pack[i] = jnp.concatenate([wide[:, :640], wide[:, 640:]], 0).astype(BF)
    small = ref_in[...].astype(F32)
    ref8[...] = jnp.concatenate([small, small[:2] * 0.0], 0).astype(BF)
    greet([at.peer(i) for i in range(1, 16)] + [at.along_x(1), at.along_x(-1), at.along_z(1), at.along_z(-1),
                                                at.along_zh(1), at.along_zh(-1)])
    sends = []

    def go(copy):
        copy.start()
        sends.append(copy)
        return copy

    steps = (1, -1)
    fulls = (full_s, full_t)
    keeps = []

    def gather_chain(h):
        full = fulls[h]
        rows = [shard_of(y + k, zl, core) for k in range(4)]
        over = [shard_of(y + k, 1 - zl, core) for k in range(4)]

        def pair(j):
            return pl.ds(2 * j, 2)

        def to_sibling(index, ref):
            go(remote(ref, ref, sib_s.at[h, index], sib_r.at[h, index], at.sibling))

        def z_send(k, src=None):
            for d in range(2):
                w = 2 * p + d
                dst = full.at[rows[k], w]
                go(remote(dst if src is None else src.at[4 * h + w], dst, gz_s.at[h, k, d], gz_r.at[h, k, d],
                          at.along_z(1 - 2 * d)))

        def z_wait(k):
            for d in range(2):
                ref = full.at[over[k], 2 * p + d]
                remote(ref, ref, gz_s.at[h, k, d], gz_r.at[h, k, d], at.along_z(1)).wait_recv()
                go(remote(ref, ref, gx_s.at[h, k, d], gx_r.at[h, k, d], at.along_x(1 - 2 * d)))
                to_sibling(7 + 2 * k + d, ref)

        def x_wait(k):
            for d in range(2):
                ref = full.at[over[k], 2 * (1 - p) + d]
                remote(ref, ref, gx_s.at[h, k, d], gx_r.at[h, k, d], at.along_x(1)).wait_recv()
                to_sibling(15 + 2 * k + d, ref)

        half = pl.ds(4 * h, 4)
        for j in range(2):
            for s, step in enumerate(steps):
                go(remote(pack.at[pl.ds(4 * h + 2 * j, 2)], full.at[me, pair(j)], y_s.at[h, s, j], y_r.at[h, s, j],
                          at.along_y(step)))
        z_send(0, pack)
        go(remote(pack.at[half], full.at[me], sib_s.at[h, 0], sib_r.at[h, 0], at.sibling))
        keeps.append(load(pack.at[half], full.at[me], loc.at[h]))
        yield
        for j in range(2):
            for s, step in enumerate(steps):
                ref = full.at[rows[(4 - step) % 4], pair(j)]
                remote(ref, ref, y_s.at[h, s, j], y_r.at[h, s, j], at.along_y(step)).wait_recv()
                if j == s:
                    go(remote(ref, ref, rel_s.at[h, j], rel_r.at[h, j], at.along_y(step)))
                to_sibling(1 + 2 * s + j, ref)
        z_send(1)
        z_send(3)
        yield
        z_wait(0)
        for j in range(2):
            ref = full.at[rows[2], pair(j)]
            remote(ref, ref, rel_s.at[h, j], rel_r.at[h, j], at.along_y(1)).wait_recv()
            to_sibling(5 + j, ref)
        z_send(2)
        yield
        z_wait(1)
        z_wait(3)
        x_wait(0)
        yield
        z_wait(2)
        x_wait(1)
        x_wait(3)
        yield
        x_wait(2)
        yield

        def sib_wait(index, ref):
            remote(ref, ref, sib_s.at[h, index], sib_r.at[h, index], at.sibling).wait_recv()

        other = [shard_of(y + k, zl, 1 - core) for k in range(4)]
        sib_wait(0, full.at[other[0]])
        for s, step in enumerate(steps):
            for j in range(2):
                sib_wait(1 + 2 * s + j, full.at[other[(4 - step) % 4], pair(j)])
        for j in range(2):
            sib_wait(5 + j, full.at[other[2], pair(j)])
        for k in range(4):
            for d in range(2):
                far = shard_of(y + k, 1 - zl, 1 - core)
                sib_wait(7 + 2 * k + d, full.at[far, 2 * p + d])
                sib_wait(15 + 2 * k + d, full.at[far, 2 * (1 - p) + d])

    def rem4(v):
        return lax.rem(v + 8, 4)

    cross = {}

    def send_cross(h, w):
        src = dws if h == 0 else dwt
        for a, zz in enumerate((oz, zl)):
            cross[h, a, w] = go(remote(src.at[1 - core, zz, w], r0.at[h, a, w], c_s.at[h, a, w], c_r.at[h, a, w],
                                       at.sibling))

    def chain(h):
        g = (dws if h == 0 else dwt).at[core]
        low, high = pl.ds(0, 48), pl.ds(48, 32)
        ys = [rem4(y + k) for k in range(4)]
        xc, zc = {}, {}

        def take(a, zz, weights):
            for w in weights:
                cross[h, a, w].wait_recv()
                g[zz, w] = add(g[zz, w], r0[h, a, w]).astype(BF)

        def x_take(k):
            for d in range(2):
                xc[k, d].wait_recv()
                w = 2 * p + d
                g[oz, w, ys[k]] = add(g[oz, w, ys[k]], rx[h, d, k]).astype(BF)
                zc[k, d] = go(remote(g.at[oz, w, ys[k]], rz.at[h, d, k], z_s.at[h, d, k], z_r.at[h, d, k],
                                     at.along_z(2 * d - 1)))

        def z_take(k):
            for d in range(2):
                zc[k, d].wait_recv()
                w = 2 * p + d
                g[zl, w, ys[k]] = add(g[zl, w, ys[k]], rz[h, d, k]).astype(BF)

        take(0, oz, (0, 3))
        yield
        take(0, oz, (1, 2))
        for k in (2, 1, 3, 0):
            for d in range(2):
                xc[k, d] = go(remote(g.at[oz, 2 * (1 - p) + d, ys[k]], rx.at[h, d, k], x_s.at[h, d, k],
                                     x_r.at[h, d, k], at.along_x(2 * d - 1)))
        take(1, zl, (0, 3, 1, 2))
        yield
        x_take(2)
        yield
        x_take(1)
        yield
        z_take(2)
        y1 = [go(remote(g.at[zl, w, ys[2]], ry1.at[h, w], y1_s.at[h, w], y1_r.at[h, w],
                        at.along_y(-1 if w < 2 else 1))) for w in range(4)]
        yield
        x_take(3)
        x_take(0)
        yield
        z_take(1)
        z_take(3)
        yield
        for w in range(4):
            y1[w].wait_recv()
            on = ys[3 if w < 2 else 1]
            g[zl, w, on] = add(g[zl, w, on], ry1[h, w]).astype(BF)
        y2 = {}
        turn = [rem4(x + 2), rem4(x + 1), rem4(x + 3), x]
        for n, w in enumerate(turn):
            for s, step in enumerate((1, -1)):
                y2[s, n] = go(remote(g.at[zl, w, ys[step % 4]], ry2.at[s, h, n], y2_s.at[s, h, n],
                                     y2_r.at[s, h, n], at.along_y(step)))
        yield
        z_take(0)
        yield

        def y_take(n):
            y2[0, n].wait_recv()
            y2[1, n].wait_recv()
            pm[h, n] = add(g[zl, turn[n], y], ry2[0, h, n], ry2[1, h, n]).astype(BF)

        y_take(0)
        a1 = [go(remote(pm.at[h, 0, part], rax1.at[h, part], a1_s.at[h, s], a1_r.at[h, s], at.along_x(step)))
              for s, (step, part) in enumerate(((1, low), (-1, high)))]
        yield
        y_take(1)
        y_take(2)
        a2 = []
        for s, (step, part) in enumerate(((1, low), (-1, high))):
            a1[s].wait_recv()
            pm[h, 1 + s, part] = add(pm[h, 1 + s, part], rax1[h, part]).astype(BF)
            a2.append(go(remote(pm.at[h, 1 + s], rax2.at[s, h], a2_s.at[h, s], a2_r.at[h, s], at.along_x(step))))
        yield
        y_take(3)
        for copy in a2:
            copy.wait_recv()
        rq[h, zh] = add(pm[h, 3], rax2[0, h], rax2[1, h]).astype(BF)
        both = ((1, low, high), (-1, high, low))
        for n in range(2):
            for s, (step, *parts) in enumerate(both):
                ref = rq.at[h, zh, parts[n]]
                go(remote(ref, ref, q_s.at[h, s, n], q_r.at[h, s, n], at.along_zh(step)))
        yield
        for s, (step, part, _) in enumerate(both):
            ref = rq.at[h, rem4(zh - step), part]
            remote(ref, ref, q_s.at[h, s, 0], q_r.at[h, s, 0], at.along_zh(step)).wait_recv()
            go(remote(ref, ref, qq_s.at[h, s], qq_r.at[h, s], at.along_zh(step)))
        yield
        for s, (step, part, rest) in enumerate(both):
            ref = rq.at[h, rem4(zh - step), rest]
            remote(ref, ref, q_s.at[h, s, 1], q_r.at[h, s, 1], at.along_zh(step)).wait_recv()
            ref = rq.at[h, rem4(zh + 2), part]
            remote(ref, ref, qq_s.at[h, s], qq_r.at[h, s], at.along_zh(step)).wait_recv()
        fin[h, x] = add(rq[h, 0], rq[h, 1], rq[h, 2], rq[h, 3]).astype(BF)
        for n in range(2):
            for s, (step, *parts) in enumerate(both):
                ref = fin.at[h, x, parts[n]]
                go(remote(ref, ref, g_s.at[h, s, n], g_r.at[h, s, n], at.along_x(step)))
        yield
        for s, (step, part, _) in enumerate(both):
            ref = fin.at[h, rem4(x - step), part]
            remote(ref, ref, g_s.at[h, s, 0], g_r.at[h, s, 0], at.along_x(step)).wait_recv()
            go(remote(ref, ref, gg_s.at[h, s], gg_r.at[h, s], at.along_x(step)))
        yield
        for s, (step, part, rest) in enumerate(both):
            ref = fin.at[h, rem4(x - step), rest]
            remote(ref, ref, g_s.at[h, s, 1], g_r.at[h, s, 1], at.along_x(step)).wait_recv()
            ref = fin.at[h, rem4(x + 2), part]
            remote(ref, ref, gg_s.at[h, s], gg_r.at[h, s], at.along_x(step)).wait_recv()
        yield

    now, later = gather_chain(0), gather_chain(1)
    next(now)
    pack_rows = frame_pack()
    buf_g[...] = dot(pack_rows, og_in[...]).astype(BF)
    masks = head_masks()
    wide = frames[...].astype(F32)
    n1 = stats(wide)[0].astype(BF)
    table[...] = position_table(32, 1280)
    next(now)
    next(now)
    for i in range(1, 16):
        go(remote(ref8, refs.at[me], ref_s.at[i], ref_r.at[i], at.peer(i)))
    refs[me] = ref8[...]
    next(later)
    next(now)
    next(now)
    next(now)
    for i in range(1, 16):
        ref = refs.at[lax.rem(me + 16 - i, 16)]
        remote(ref, ref, ref_s.at[i], ref_r.at[i], at.peer(i)).wait_recv()
    for _ in now:
        pass
    keeps[0].wait()
    ref = dot(ref_unpack(96, 128), refs[...].astype(F32).reshape(128, 1280).astype(BF)).astype(BF)
    q = dot(n1, full_s[:, 0].reshape(1280, 640)).astype(BF)
    w = full_s[:, 1].reshape(1280, 640)
    k, rk = dot(n1, w).astype(BF), dot(ref, w).astype(BF)
    next(later)
    w = full_s[:, 2].reshape(1280, 640)
    v, rv = dot(n1, w).astype(BF), dot(ref, w).astype(BF)
    for i, part in enumerate((q, k, v)):
        qkv[i] = part
    rkv[0] = rk
    rkv[1] = rv
    outs = []
    for a in range(2):
        rows = slice(96 * a, 96 * a + 96)
        keys = jnp.concatenate([k[rows], rk], 0)
        values = jnp.concatenate([v[rows], rv], 0)
        probs = softmax(stack_heads(q[rows], masks), keys).astype(BF)
        outs.append(merge_heads(dot(probs, values), masks))
        next(later)
    o = jnp.concatenate(outs, 0).astype(BF)
    o_in[...] = o
    left, right = wide_output(full_s[:, 3])
    h1 = (wide + jnp.concatenate([dot(o, left), dot(o, right)], 1)).astype(BF)
    h1_in[...] = h1
    buf_b[...] = dot(pack_rows, h1).astype(BF)
    copies = exchange_start(at, buf_b, h1r, ex_s.at[0], ex_r.at[0])
    to_owner = exchange_start(at, buf_g, ogr, ex_s.at[1], ex_r.at[1])
    for _ in later:
        pass
    for keep in keeps[1:]:
        keep.wait()
    for copy in copies:
        copy.wait_recv()
    unpack, t_pack = token_unpack(), token_pack()
    h1 = dot(unpack, h1r[...])
    centred, inverse = stats(h1)
    n2 = (centred + jnp.concatenate([table[...]] * 6, 0)).astype(BF)
    parts = []
    for i in range(3):
        parts.append(dot(n2, full_t[:, i].reshape(1280, 640)).astype(BF))
    q, k, v = parts
    r, c = iota((768, 192), 0), iota((768, 192), 1)
    r = jnp.where(r >= 384, r - 384, r)
    r = jnp.where(r >= 192, r - 192, r)
    same = lax.shift_right_logical(r, 5) == lax.shift_right_logical(c, 5)
    qs = stack_heads(q, masks)
    probs = softmax(qs, k, same)
    pb = probs.astype(BF)
    o2 = merge_heads(dot(pb, v), masks).astype(BF)
    buf_o[...] = dot(t_pack, o2).astype(BF)
    to_frame = exchange_start(at, buf_o, o2r, ex_s.at[2], ex_r.at[2])
    left, right = wide_output(full_t[:, 3])
    for copy in to_owner:
        copy.wait_recv()
    og = dot(unpack, ogr[...]).astype(BF)
    go2 = (dot(og[:, :640], left, 1, 1) + dot(og[:, 640:], right, 1, 1)).astype(BF)
    gs = stack_heads(go2, masks)
    eb = score_back(probs, gs, v)
    gq = merge_heads(dot(eb, k), masks).astype(BF)
    gk = dot(eb, qs, 0, 0).astype(BF)
    gv = dot(pb, gs, 0, 0).astype(BF)
    grads = (gq, gk, gv)
    gn = dot(gq, full_t[:, 0].reshape(1280, 640), 1, 1)
    for i in (1, 2):
        gn = gn + dot(grads[i], full_t[:, i].reshape(1280, 640), 1, 1)
    gh = (og.astype(F32) + stats_back(centred, inverse, gn)).astype(BF)
    buf[...] = dot(t_pack, gh).astype(BF)
    to_frame += exchange_start(at, buf, backr, ex_s.at[3], ex_r.at[3])
    for i in range(3):
        store_term(dwt, i, dot(n2, grads[i], 0, 0))
        send_cross(1, i)
    store_term(dwt, 3, pack_output(dot(o2, og[:, :640], 0, 0), dot(o2, og[:, 640:], 0, 0)))
    send_cross(1, 3)
    early = chain(1)
    next(early)
    for copy in to_frame:
        copy.wait_recv()
    f_unpack = frame_unpack()
    gh = dot(f_unpack, backr[...]).astype(BF)
    next(early)
    left, right = wide_output(full_s[:, 3])
    go_ = (dot(gh[:, :640], left, 1, 1) + dot(gh[:, 640:], right, 1, 1)).astype(BF)
    rk, rv = rkv[0], rkv[1]
    gq, gk, gv = [], [], []
    grk = grv = None
    for a in range(2):
        rows = slice(96 * a, 96 * a + 96)
        keys = jnp.concatenate([qkv[1, rows], rk], 0)
        values = jnp.concatenate([qkv[2, rows], rv], 0)
        qs = stack_heads(qkv[0, rows], masks)
        gs = stack_heads(go_[rows], masks)
        probs = softmax(qs, keys)
        eb = score_back(probs, gs, values)
        gq.append(merge_heads(dot(eb, keys), masks))
        gkeys = dot(eb, qs, 0, 0)
        gvalues = dot(probs.astype(BF), gs, 0, 0)
        gk.append(gkeys[:96])
        gv.append(gvalues[:96])
        grk = gkeys[96:] if grk is None else grk + gkeys[96:]
        grv = gvalues[96:] if grv is None else grv + gvalues[96:]
        next(early)
        next(early)
    gq, gk, gv = (jnp.concatenate(g, 0).astype(BF) for g in (gq, gk, gv))
    grk, grv = grk.astype(BF), grv.astype(BF)
    centred, inverse = stats(frames[...].astype(F32))
    n1 = centred.astype(BF)
    o = o_in[...]
    store_term(dws, 3, pack_output(dot(o, gh[:, :640], 0, 0), dot(o, gh[:, 640:], 0, 0)))
    send_cross(0, 3)
    store_term(dws, 0, dot(n1, gq, 0, 0))
    send_cross(0, 0)
    store_term(dws, 1, dot(n1, gk, 0, 0) + dot(ref, grk, 0, 0))
    send_cross(0, 1)
    late = chain(0)
    store_term(dws, 2, dot(n1, gv, 0, 0) + dot(ref, grv, 0, 0))
    send_cross(0, 2)
    next(late)
    next(late)
    spread = ref_unpack(128, 96, True)
    gr[:, :, :640] = dot(spread, grk).reshape(16, 8, 640).astype(BF)
    gr[:, :, 640:] = dot(spread, grv).reshape(16, 8, 640).astype(BF)
    rgr[me] = gr[me]
    next(early)
    for i in range(1, 16):
        to = lax.rem(me + i, 16)
        go(remote(gr.at[to], rgr.at[me], e_s.at[i], e_r.at[i], at.peer(i)))

    def finish_rows():
        gn = None
        for n, (i, g) in enumerate(((0, gq), (1, gk), (2, gv))):
            term = dot(g, full_s[:, n].reshape(1280, 640), 1, 1)
            gn = term if gn is None else gn + term
        fg_o[...] = (gh.astype(F32) + stats_back(centred, inverse, gn)).astype(BF)

    def finish_out():
        left, right = wide_output(full_t[:, 3])
        o2 = dot(f_unpack, o2r[...]).astype(BF)
        out_o[...] = (h1_in[...].astype(F32) + jnp.concatenate([dot(o2, left), dot(o2, right)], 1)).astype(BF)

    def finish_ref():
        for i in range(1, 16):
            got = rgr.at[lax.rem(me + 16 - i, 16)]
            remote(got, got, e_s.at[i], e_r.at[i], at.peer(i)).wait_recv()
        total = rgr[0].astype(F32)
        for i in range(1, 16):
            total = total + rgr[i].astype(F32)
        total = total.astype(BF)
        rg[...] = (dot(total[:, :640], full_s[:, 1].reshape(1280, 640), 1, 1)
                   + dot(total[:, 640:], full_s[:, 2].reshape(1280, 640), 1, 1)).astype(BF)

    work = {"A": finish_rows, "B": finish_out, "C": finish_ref}
    for step in ORDER:
        if step in work:
            work[step]()
        else:
            next(early if step == "T" else late)
    for copy in copies + to_owner + to_frame + sends:
        copy.wait_send()


def whole(frames, ref_in, og, weights):
    dma = pltpu.SemaphoreType.DMA
    s = jax.ShapeDtypeStruct
    v = pltpu.VMEM
    b = (80, 640)
    wide = v((256, 1280), BF)
    return pl.pallas_call(
        whole_kernel,
        out_shape=(s((192, 1280), BF), s((192, 1280), BF), s((8, 1280), BF), s((2, 4) + b, BF)),
        in_specs=[VM] * 11,
        out_specs=(VM,) * 4,
        scratch_shapes=[v((8,) + b, BF), v((8, 1280), BF), v((16, 4) + b, BF), v((16, 4) + b, BF),
                        v((16, 8, 1280), BF), v((3, 192, 640), BF), v((2, 96, 640), BF), v((192, 640), BF),
                        v((192, 1280), BF), v((32, 1280), F32), wide, wide, wide, wide, v((256, 640), BF), v((256, 640), BF), wide, wide,
                        v((2, 2, 4, 4) + b, BF), v((2, 2, 4, 4) + b, BF), v((2, 2, 4, 4) + b, BF),
                        v((2, 2, 4) + b, BF), v((2, 2, 4) + b, BF), v((2, 4) + b, BF), v((2, 2, 4) + b, BF),
                        v((2, 4) + b, BF), v((2,) + b, BF), v((2, 2) + b, BF), v((2, 4) + b, BF),
                        v((16, 8, 1280), BF), v((16, 8, 1280), BF)]
        + [dma((2, 23))] * 2 + [dma((2, 2, 2))] * 2 + [dma((2, 2))] * 2 + [dma((2, 4, 2))] * 4 + [dma((16,))] * 2
        + [dma((4, 16))] * 2 + [dma((2,))]
        + [dma((2, 2, 4))] * 6 + [dma((2, 4))] * 2 + [dma((2, 2, 4))] * 2 + [dma((2, 2))] * 4 + [dma((2, 2, 2))] * 2
        + [dma((2, 2))] * 2 + [dma((2, 2, 2))] * 2 + [dma((2, 2))] * 2 + [dma((16,))] * 2,
        compiler_params=pltpu.CompilerParams(collective_id=0, has_side_effects=True,
                                             vmem_limit_bytes=67043328),
        name="whole",
    )(frames, ref_in, og, *weights)


def finish_kernel(out, fg, rg, fin, out_o, fg_o, rg_o, *totals):
    out_o[...] = out[...]
    fg_o[...] = fg[...]
    rg_o[...] = rg[...].astype(F32)[:6].astype(BF)
    for h in range(2):
        for w in range(3):
            totals[4 * h + w][...] = fin[h, w].astype(F32)
        wide = fin[h, 3].astype(F32)
        totals[4 * h + 3][:, :640] = wide[:40]
        totals[4 * h + 3][:, 640:] = wide[40:]


def finish(out, fg, rg, fin):
    s = jax.ShapeDtypeStruct
    tall, flat = s((80, 640), F32), s((40, 1280), F32)
    return pl.pallas_call(
        finish_kernel,
        out_shape=(s((192, 1280), BF), s((192, 1280), BF), s((6, 1280), BF)) + (tall, tall, tall, flat) * 2,
        in_specs=[VM] * 4, out_specs=(VM,) * 11, name="write_outputs",
    )(out, fg, rg, fin)

def per_device(frames_in, ref_feats, out_grad, *weights):
    frames, grads = frames_in.reshape(192, 1280), out_grad.reshape(192, 1280)
    results = whole(frames, ref_feats[0], grads, weights)
    out, frames_grad, rg, *totals = finish(*results)
    return (out.reshape(frames_in.shape), frames_grad.reshape(frames_in.shape), rg[None], *totals)


def solution(mesh):
    rows, refs, weight = P("clip", "frame", None, None), P("clip", "frame", None), P("frame", None)
    return jax.shard_map(
        per_device, mesh=mesh, in_specs=(rows, refs, rows) + (weight,) * 8,
        out_specs=(rows, rows, refs) + (weight,) * 8, check_vma=False)
```
